256 devices in a mesh: view: 16 (over x, z_lo), slab: 16 (over z_hi, y, core).
Axes of the slice: x: 4, y: 4, z: 8 (z_hi: 2, z_lo: 4; z = z_hi * 4 + z_lo), core: 2. Of those that a mesh axis runs over, the one named last changes fastest.
Arguments:
- estimate: float32 [256, 64, 512], P('slab', 'view'), may hold values from 0.5 to 2
- observed: float32 [16, 256, 64, 512], P('view', 'slab'), may hold values from 0.5 to 2
- psf_z: float32 [16, 3, 31], P('view'), may hold values from 0.01 to 1
- psf_y: float32 [16, 3, 31], P('view'), may hold values from 0.01 to 1
- psf_x: float32 [16, 3, 31], P('view'), may hold values from 0.01 to 1
Outputs:
- updated: float32 [256, 64, 512], P('slab', 'view')
The draws below stay inside these ranges and needn't reach their ends.
All inputs are finite; a program needn't handle non-finite values.
Results may differ from the reference program's by a relative error of at most 0.00018.
Values sent between devices are 32-bit elements; how exact they have to be, the bound alone decides.
A program may use at most 128 MiB of HBM per device.

```python
import math
import jax
import jax.numpy as jnp
from jax import lax

Y = 64
X = 512
RANK = 3
TAPS = 31
HALF = 15
ITERS = 1
VIEWS = 16
NZ = 256


def block_levels(rng, dims, cuts, low, largest):
    gain, own = 1.0, jax.random.fold_in(rng, 6)
    for position, parts in cuts:
        draws = jnp.exp(jax.random.uniform(jax.random.fold_in(own, position), (parts,), jnp.float32, low / len(cuts), largest / len(cuts)))
        gain = gain * jnp.repeat(draws, dims[position] // parts).reshape([-1 if axis == position else 1 for axis in range(len(dims))])
    return gain


def setup_inputs(seed: int = 0) -> dict:
    streams_of = jax.random.split(jax.random.key(seed), 6)
    return {
        "estimate": jnp.clip(jnp.exp(math.log(2.0) - 1.3862944 * jax.random.uniform(streams_of[0], (NZ, Y, X), jnp.float32) ** block_levels(streams_of[0], (NZ, Y, X), ((0, 16), (1, 16)), -0.2, 0.2)), 0.5, 2.0),
        "observed": jnp.clip(jnp.exp(math.log(2.0) - 1.3862944 * jax.random.uniform(streams_of[1], (VIEWS, NZ, Y, X), jnp.float32) ** block_levels(streams_of[1], (VIEWS, NZ, Y, X), ((0, 16), (1, 16)), -0.2, 0.2)), 0.5, 2.0),
        "psf_z": jnp.clip(jnp.exp(math.log(1.0) - 4.6051702 * jax.random.uniform(streams_of[2], (VIEWS, RANK, TAPS), jnp.float32) ** block_levels(streams_of[2], (VIEWS, RANK, TAPS), ((0, 16),), -0.2, 0.2)), 0.01, 1.0),
        "psf_y": jnp.clip(jnp.exp(math.log(1.0) - 4.6051702 * jax.random.uniform(streams_of[3], (VIEWS, RANK, TAPS), jnp.float32) ** block_levels(streams_of[3], (VIEWS, RANK, TAPS), ((0, 16),), -0.2, 0.2)), 0.01, 1.0),
        "psf_x": jnp.clip(jnp.exp(math.log(1.0) - 4.6051702 * jax.random.uniform(streams_of[4], (VIEWS, RANK, TAPS), jnp.float32) ** block_levels(streams_of[4], (VIEWS, RANK, TAPS), ((0, 16),), -0.2, 0.2)), 0.01, 1.0),
    }


def band_matrix(taps, count):
    rows = jnp.arange(count, dtype=jnp.int32)[:, None]
    cols = jnp.arange(count, dtype=jnp.int32)[None, :]
    offset = (cols - rows + HALF).astype(jnp.int32)
    valid = (offset >= 0) & (offset < TAPS)
    picked = taps[:, jnp.clip(offset, 0, TAPS - 1)]
    return jnp.where(valid[None], picked, jnp.zeros_like(picked))


def block_tables(taps, block_size):
    rows = jnp.arange(block_size, dtype=jnp.int32)[:, None]
    cols = jnp.arange(block_size + 2 * HALF, dtype=jnp.int32)[None, :]
    offset = (cols - rows).astype(jnp.int32)
    valid = (offset >= 0) & (offset < TAPS)
    picked = taps[:, jnp.clip(offset, 0, TAPS - 1)]
    full = jnp.where(valid[None], picked, jnp.zeros_like(picked))
    centre = full[:, :, HALF:HALF + block_size]
    edges = jnp.concatenate([full[:, :, :HALF], full[:, :, HALF + block_size:]], 2)
    return centre, edges


def x_blur(volume, centre, edges):
    high = lax.Precision.HIGHEST
    depth, height, width = volume.shape
    block_size = centre.shape[0]
    block_count = width // block_size
    blocks = volume.reshape(depth, height, block_count, block_size)
    zero_edge = jnp.zeros((depth, height, 1, HALF), volume.dtype)
    left_rim = jnp.concatenate([zero_edge, blocks[:, :, :block_count - 1, block_size - HALF:]], 2)
    right_rim = jnp.concatenate([blocks[:, :, 1:, :HALF], zero_edge], 2)
    both_rims = jnp.concatenate([left_rim, right_rim], 3)
    result = jnp.einsum('zynj,ij->zyni', blocks, centre, precision=high)
    result = result + jnp.einsum('zynj,ij->zyni', both_rims, edges, precision=high)
    return result.reshape(depth, height, width)


def depth_forward(volume, taps):
    padded = jnp.pad(volume, ((HALF, HALF), (0, 0), (0, 0)))
    depth = volume.shape[0]
    total = jnp.zeros_like(volume)
    for k in range(TAPS):
        total = total + taps[k] * padded[k:k + depth]
    return total


def depth_back(volume, taps):
    padded = jnp.pad(volume, ((HALF, HALF), (0, 0), (0, 0)))
    depth = volume.shape[0]
    total = jnp.zeros_like(volume)
    for k in range(TAPS):
        total = total + taps[k] * padded[2 * HALF - k:2 * HALF - k + depth]
    return total


def view_log(field, seen, taps_z, taps_y, taps_x):
    high = lax.Precision.HIGHEST
    block_size = min(128, field.shape[2])
    centre, edges = block_tables(taps_x, block_size)
    centre_back, edges_back = block_tables(taps_x[:, ::-1], block_size)
    mat_y = band_matrix(taps_y, field.shape[1])

    def forward(total, items):
        cen, edg, by, az = items
        part = x_blur(field, cen, edg)
        part = jnp.einsum('zjx,ij->zix', part, by, precision=high)
        return total + depth_forward(part, az), None

    blurred, _ = lax.scan(forward, jnp.zeros_like(field), (centre, edges, mat_y, taps_z))
    ratio = seen / blurred

    def backward(total, items):
        cen, edg, by, az = items
        part = x_blur(ratio, cen, edg)
        part = jnp.einsum('zix,ij->zjx', part, by, precision=high)
        return total + depth_back(part, az), None

    back, _ = lax.scan(backward, jnp.zeros_like(field), (centre_back, edges_back, mat_y, taps_z))
    return jnp.log(back)


def reference(estimate, observed, psf_z, psf_y, psf_x):
    field = estimate
    for step in range(ITERS):
        def accumulate(total, items):
            seen, taps_z, taps_y, taps_x = items
            return total + view_log(field, seen, taps_z, taps_y, taps_x), None

        logsum, _ = lax.scan(accumulate, jnp.zeros_like(field), (observed, psf_z, psf_y, psf_x))
        field = field * jnp.exp(logsum)
    return field
```

```python
import functools

import jax
import jax.numpy as jnp
from jax import lax
from jax.experimental import pallas as pl
from jax.experimental.pallas import tpu as pltpu
from jax.sharding import PartitionSpec as P

RANK = 3
TAPS = 31
HALF = 15
F32, BF16 = jnp.float32, jnp.bfloat16


def split(x):
    hi = x.astype(BF16)
    return hi, (x - hi.astype(F32)).astype(BF16)


def pick(code, count, tap):
    def one(k, acc):
        return jnp.where(code == k, tap(k), acc)

    return lax.fori_loop(0, count, one, jnp.zeros(code.shape, F32))


def iotas(shape):
    return [lax.broadcasted_iota(jnp.int32, shape, d) for d in range(2)]


def build_tables(pz, py, px, wz, wy, cx, ex, back):
    def tap_of(ref):
        return lambda k: ref[k // 32, k % 32]

    row, col = iotas((48, 96))
    p = jnp.where(col < 48, col, col - 48)
    d = (row % 16) - p + 31 if back else p - (row % 16) - 1
    code = jnp.where((d >= 0) & (d < TAPS), (row // 16) * 32 + d, -1)
    hi, lo = split(pick(code, RANK * 32, tap_of(pz)))
    wz[0:48, :] = hi
    wz[48:96, :] = jnp.where(col < 48, lo.astype(F32), 0.0).astype(BF16)

    row, col = iotas((64, 384))
    c = jnp.where(col < 192, col, col - 192)
    d = row - (c % 64) + HALF if back else (c % 64) - row + HALF
    code = jnp.where((d >= 0) & (d < TAPS), (c // 64) * 32 + d, -1)
    hi, lo = split(pick(code, RANK * 32, tap_of(py)))
    wy[0:64, :] = hi
    wy[64:128, :] = jnp.where(col < 192, lo.astype(F32), 0.0).astype(BF16)

    row, col = iotas((128, 128))
    d = col - row + HALF if back else row - col + HALF
    ring = lax.rem(d + 128, 128)
    near = (d >= 0) & (d < TAPS)
    zero = jnp.zeros((128, 128), BF16)
    for r in range(RANK):
        full = pick(ring, TAPS, lambda k: px[r, k])
        for ref, keep in ((cx, near), (ex, jnp.logical_not(near))):
            hi, lo = split(jnp.where(keep, full, 0.0))
            ref[r, 0:128, 0:128] = hi
            ref[r, 0:128, 128:256] = lo
            ref[r, 128:256, 0:128] = hi
            ref[r, 128:256, 128:256] = zero


def dot(a, b):
    return jnp.dot(a, b, preferred_element_type=F32)


def z_stage(src, wz, thi, tlo, unroll=4):
    def one(y, _):
        hi, lo = split(src[y])
        o = dot(wz[...], jnp.concatenate([hi, lo], axis=0))
        hi, lo = split(o[:48] + o[48:])
        thi[y] = hi
        tlo[y] = lo
        return 0

    lax.fori_loop(0, 64, one, 0, unroll=unroll)


def x_stage(thi, tlo, cx, ex, xo, rows=8):
    m = rows * 16
    low = lax.broadcasted_iota(jnp.int32, (m, 128), 1) < 64

    for r in range(RANK):

        def one(c, _):
            ys = pl.ds(c * rows, rows)
            hi = thi[ys, 16 * r : 16 * r + 16, :].reshape(m, 512)
            lo = tlo[ys, 16 * r : 16 * r + 16, :].reshape(m, 512)
            h = [hi[:, 128 * b : 128 * b + 128] for b in range(4)]
            l = [lo[:, 128 * b : 128 * b + 128] for b in range(4)]
            out = []
            for b in range(4):
                o = dot(jnp.concatenate([h[b], l[b]], axis=1), cx[r])
                out.append(o[:, :128] + o[:, 128:])
            for b in range(3):
                ph = jnp.where(low, h[b + 1], h[b])
                pll = jnp.where(low, l[b + 1], l[b])
                o = dot(jnp.concatenate([ph, pll], axis=1), ex[r])
                e = o[:, :128] + o[:, 128:]
                out[b] = out[b] + jnp.where(low, 0.0, e)
                out[b + 1] = out[b + 1] + jnp.where(low, e, 0.0)
            rr = pl.ds(r * 1024 + c * m, m)
            for b in range(4):
                xo[b, rr, :] = out[b]
            return 0

        lax.fori_loop(0, 64 // rows, one, 0)


def y_stage(xo, wy, finish, lo=0, hi=16):
    def one(z, _):
        planes = []
        for r in range(RANK):
            parts = [xo[b, pl.ds(r * 1024 + z, 64, stride=16), :] for b in range(4)]
            planes.append(jnp.concatenate(parts, axis=1))
        h, l = split(jnp.concatenate(planes, axis=0))
        o = dot(wy[...], jnp.concatenate([h, l], axis=0))
        finish(z, o[:64] + o[64:])
        return 0

    lax.fori_loop(lo, hi, one, 0)


TABLES = [
    pltpu.VMEM((96, 96), BF16),
    pltpu.VMEM((128, 384), BF16),
    pltpu.VMEM((3, 256, 256), BF16),
    pltpu.VMEM((3, 256, 256), BF16),
]
WORK = [
    pltpu.VMEM((64, 48, 512), BF16),
    pltpu.VMEM((64, 48, 512), BF16),
    pltpu.VMEM((4, 3072, 128), F32),
]


def forward_kernel(pz, py, px, fld, obs, out, wz, wy, cx, ex, thi, tlo, xo, rat):
    build_tables(pz, py, px, wz, wy, cx, ex, False)
    z_stage(fld, wz, thi, tlo)
    x_stage(thi, tlo, cx, ex, xo)

    def finish(z, blurred):
        ratio = obs[z] / blurred
        for b in range(4):
            rat[b, pl.ds(z, 64, stride=16), :] = ratio[:, 128 * b : 128 * b + 128]

    y_stage(xo, wy, finish)
    for b in range(4):
        out[:, :, 128 * b : 128 * b + 128] = rat[b].reshape(64, 16, 128)


def backward_kernel(pz, py, px, rat, out, wz, wy, cx, ex, thi, tlo, xo):
    build_tables(pz, py, px, wz, wy, cx, ex, True)
    z_stage(rat, wz, thi, tlo)
    x_stage(thi, tlo, cx, ex, xo)

    def finish(z, back):
        out[z] = jnp.log(back)

    y_stage(xo, wy, finish)


SMEM = pl.BlockSpec(memory_space=pltpu.SMEM)
VM = pl.BlockSpec(memory_space=pltpu.VMEM)
PARAMS = dict(vmem_limit_bytes=60 << 20)


def forward(pz, py, px, fld, obs):
    return pl.pallas_call(
        forward_kernel,
        out_shape=jax.ShapeDtypeStruct((64, 16, 512), F32),
        in_specs=[SMEM] * 3 + [VM] * 2,
        out_specs=VM,
        scratch_shapes=TABLES + WORK + [pltpu.VMEM((4, 1024, 128), F32)],
        compiler_params=pltpu.CompilerParams(**PARAMS),
        name="forward",
    )(pz, py, px, fld, obs)


def backward(pz, py, px, rat):
    return pl.pallas_call(
        backward_kernel,
        out_shape=jax.ShapeDtypeStruct((16, 64, 512), F32),
        in_specs=[SMEM] * 3 + [VM],
        out_specs=VM,
        scratch_shapes=TABLES + WORK,
        compiler_params=pltpu.CompilerParams(**PARAMS),
        name="backward",
    )(pz, py, px, rat)


def neighbours(shard):
    peers = lax.axis_size("slab")
    up = [(i, i + 1) for i in range(peers - 1)]
    down = [(j, i) for i, j in up]
    before = lax.ppermute(shard, "slab", up)
    after = lax.ppermute(shard, "slab", down)
    return jnp.concatenate([before, shard, after], axis=1)


def padded(taps):
    return jnp.pad(taps, ((0, 0), (0, 1)))


def local(estimate, observed, psf_z, psf_y, psf_x):
    pz, py, px = (padded(t[0]) for t in (psf_z, psf_y, psf_x))
    mine = jnp.swapaxes(estimate, 0, 1)
    copies = jnp.broadcast_to(mine, (lax.axis_size("view"), *mine.shape))
    field = lax.all_to_all(copies, "view", 0, 0, tiled=True).reshape(64, 16, 512)
    ratio = forward(pz, py, px, neighbours(field), observed[0])
    logs = backward(pz, py, px, neighbours(ratio))
    blocks = jnp.moveaxis(logs.reshape(16, 16, 4, 512), 1, 0)
    share = jnp.sum(lax.all_to_all(blocks, "view", 0, 0, tiled=True), axis=0)
    return estimate * jnp.exp(share)


def solution(mesh):
    placed = (
        P("slab", "view", None),
        P("view", "slab", None, None),
        P("view", None, None),
        P("view", None, None),
        P("view", None, None),
    )
    return jax.shard_map(
        local, mesh=mesh, in_specs=placed, out_specs=P("slab", "view", None), check_vma=False
    )
```

```python
import functools

import jax
import jax.numpy as jnp
from jax import lax
from jax.experimental import pallas as pl
from jax.experimental.pallas import tpu as pltpu
from jax.sharding import PartitionSpec as P

RANK = 3
TAPS = 31
HALF = 15
F32, BF16 = jnp.float32, jnp.bfloat16


def split(x):
    hi = x.astype(BF16)
    return hi, (x - hi.astype(F32)).astype(BF16)


def pick(code, count, tap):
    def one(k, acc):
        return jnp.where(code == k, tap(k), acc)

    return lax.fori_loop(0, count, one, jnp.zeros(code.shape, F32))


def iotas(shape):
    return [lax.broadcasted_iota(jnp.int32, shape, d) for d in range(2)]


def build_tables(pz, py, px, wz, wy, cx, ex, back):
    def tap_of(ref):
        return lambda k: ref[k // 32, k % 32]

    row, col = iotas((48, 96))
    p = jnp.where(col < 48, col, col - 48)
    d = (row % 16) - p + 31 if back else p - (row % 16) - 1
    code = jnp.where((d >= 0) & (d < TAPS), (row // 16) * 32 + d, -1)
    hi, lo = split(pick(code, RANK * 32, tap_of(pz)))
    wz[0:48, :] = hi
    wz[48:96, :] = jnp.where(col < 48, lo.astype(F32), 0.0).astype(BF16)

    row, col = iotas((64, 384))
    c = jnp.where(col < 192, col, col - 192)
    d = row - (c % 64) + HALF if back else (c % 64) - row + HALF
    code = jnp.where((d >= 0) & (d < TAPS), (c // 64) * 32 + d, -1)
    hi, lo = split(pick(code, RANK * 32, tap_of(py)))
    wy[0:64, :] = hi
    wy[64:128, :] = jnp.where(col < 192, lo.astype(F32), 0.0).astype(BF16)

    row, col = iotas((128, 128))
    d = col - row + HALF if back else row - col + HALF
    ring = lax.rem(d + 128, 128)
    near = (d >= 0) & (d < TAPS)
    zero = jnp.zeros((128, 128), BF16)
    for r in range(RANK):
        full = pick(ring, TAPS, lambda k: px[r, k])
        for ref, keep in ((cx, near), (ex, jnp.logical_not(near))):
            hi, lo = split(jnp.where(keep, full, 0.0))
            ref[r, 0:128, 0:128] = hi
            ref[r, 0:128, 128:256] = lo
            ref[r, 128:256, 0:128] = hi
            ref[r, 128:256, 128:256] = zero


def dot(a, b):
    return jnp.dot(a, b, preferred_element_type=F32)


def z_stage(src, wz, thi, tlo, unroll=4):
    def one(y, _):
        hi, lo = split(jnp.concatenate([src[b, y] for b in range(4)], axis=1))
        o = dot(wz[...], jnp.concatenate([hi, lo], axis=0))
        hi, lo = split(o[:48] + o[48:])
        thi[y] = hi
        tlo[y] = lo
        return 0

    lax.fori_loop(0, 64, one, 0, unroll=unroll)


def x_stage(thi, tlo, cx, ex, xo, rows=8):
    m = rows * 16
    low = lax.broadcasted_iota(jnp.int32, (m, 128), 1) < 64

    for r in range(RANK):

        def one(c, _):
            ys = pl.ds(c * rows, rows)
            hi = thi[ys, 16 * r : 16 * r + 16, :].reshape(m, 512)
            lo = tlo[ys, 16 * r : 16 * r + 16, :].reshape(m, 512)
            h = [hi[:, 128 * b : 128 * b + 128] for b in range(4)]
            l = [lo[:, 128 * b : 128 * b + 128] for b in range(4)]
            out = []
            for b in range(4):
                o = dot(jnp.concatenate([h[b], l[b]], axis=1), cx[r])
                out.append(o[:, :128] + o[:, 128:])
            for b in range(3):
                ph = jnp.where(low, h[b + 1], h[b])
                pll = jnp.where(low, l[b + 1], l[b])
                o = dot(jnp.concatenate([ph, pll], axis=1), ex[r])
                e = o[:, :128] + o[:, 128:]
                out[b] = out[b] + jnp.where(low, 0.0, e)
                out[b + 1] = out[b + 1] + jnp.where(low, e, 0.0)
            rr = pl.ds(r * 1024 + c * m, m)
            for b in range(4):
                xo[b, rr, :] = out[b]
            return 0

        lax.fori_loop(0, 64 // rows, one, 0)


def y_stage(xo, wy, finish, lo=0, hi=16):
    def one(z, _):
        planes = []
        for r in range(RANK):
            parts = [xo[b, pl.ds(r * 1024 + z, 64, stride=16), :] for b in range(4)]
            planes.append(jnp.concatenate(parts, axis=1))
        h, l = split(jnp.concatenate(planes, axis=0))
        o = dot(wy[...], jnp.concatenate([h, l], axis=0))
        finish(z, o[:64] + o[64:])
        return 0

    lax.fori_loop(lo, hi, one, 0)


SLABS, GROUP = 16, 4
MESH = pl.DeviceIdType.MESH


def remote(src, dst, send, recv, device):
    return pltpu.make_async_remote_copy(
        src_ref=src, dst_ref=dst, send_sem=send, recv_sem=recv, device_id=device, device_id_type=MESH
    )


def z_rows(src, wz, thi, tlo, start, count):
    for i in range(count):
        y = start + i
        hi, lo = split(src[y])
        o = dot(wz[...], jnp.concatenate([hi, lo], axis=0))
        hi, lo = split(o[:48] + o[48:])
        thi[y] = hi
        tlo[y] = lo


def kernel(
    pz, py, px, est, obs_hbm, out,
    fld, rat, obs, thi, tlo, xo, logs, xin, zout, zin,
    wzf, wyf, cxf, exf, wzb, wyb, cxb, exb,
    obs_sem, main_recv, lo_recv, hi_recv, cross_recv,
    zsend, xsend, upsend, dnsend, csend, czsend, cxsend,
    rup_send, rdn_send, rlo_recv, rhi_recv,
    sx_send, sx_recv, sz_send, sz_recv,
):
    v, s = lax.axis_index("view"), lax.axis_index("slab")
    x, zl = lax.div(v, GROUP), lax.rem(v, GROUP)
    zpeer = [x * GROUP + lax.rem(zl + i, GROUP) for i in range(1, GROUP)]
    xs = [lax.rem(x + i, GROUP) for i in (1, 3, 2)]
    xpeer = [a * GROUP + zl for a in xs]
    lower, upper = s > 0, s < SLABS - 1
    cross_lo, cross_hi = s == SLABS // 2, s == SLABS // 2 - 1
    cross = jnp.logical_or(cross_lo, cross_hi)
    near_lo = jnp.logical_and(lower, jnp.logical_not(cross_lo))
    near_hi = jnp.logical_and(upper, jnp.logical_not(cross_hi))
    my_off = pl.multiple_of(jnp.where(cross_lo, 0, 32), 16)
    far_off = pl.multiple_of(jnp.where(cross_lo, 32, 0), 16)
    far_slab = jnp.where(cross_lo, s - 1, s + 1)

    def block(shard, off):
        return fld.at[pl.ds(shard * 4, 4), pl.ds(off, 16), :]

    for q in range(4):
        fld[v * 4 + q, 16:32, :] = est[:, q, :]

    barrier = pltpu.get_barrier_semaphore()
    for peer in zpeer + xpeer:
        pl.semaphore_signal(barrier, inc=1, device_id=(peer, s), device_id_type=MESH)

    @pl.when(lower)
    def _():
        pl.semaphore_signal(barrier, inc=1, device_id=(v, s - 1), device_id_type=MESH)

    @pl.when(upper)
    def _():
        pl.semaphore_signal(barrier, inc=1, device_id=(v, s + 1), device_id_type=MESH)

    pl.semaphore_wait(barrier, 6 + jnp.where(lower, 1, 0) + jnp.where(upper, 1, 0))

    def to_z(shard, off, i, sends, recv):
        return remote(block(shard, off), block(shard, off), sends.at[i], recv.at[shard], (zpeer[i], s))

    def to_x(shard, off, k, i, sends, recv):
        return remote(block(shard, off), block(shard, off), sends.at[k, i], recv.at[shard], (xpeer[i], s))

    def to_up(shard, k):
        return remote(block(shard, 16), block(shard, 0), upsend.at[k], lo_recv.at[shard], (v, s + 1))

    def to_dn(shard, k):
        return remote(block(shard, 16), block(shard, 32), dnsend.at[k], hi_recv.at[shard], (v, s - 1))

    def to_far():
        return remote(block(v, 16), block(v, far_off), csend.at[0], cross_recv.at[v], (v, far_slab))

    def halo(shard, k):
        @pl.when(near_hi)
        def _():
            to_up(shard, k).start()

        @pl.when(near_lo)
        def _():
            to_dn(shard, k).start()

    near = [v] + zpeer
    groups = [near] + [[xs[j] * GROUP + lax.rem(zl + i, GROUP) for i in range(GROUP)] for j in range(3)]

    @pl.when(cross)
    def _():
        to_far().start()

    for i in range(3):
        to_z(v, 16, i, zsend, main_recv).start()
    for i in range(3):
        to_x(v, 16, 0, i, xsend, main_recv).start()
    halo(v, 0)
    load = pltpu.make_async_copy(obs_hbm, obs, obs_sem.at[0])
    load.start()

    @pl.when(s == 0)
    def _():
        fld[:, 0:16, :] = jnp.zeros((64, 16, 512), F32)
        rat[:, :, 0:16, :] = jnp.zeros((4, 64, 16, 128), F32)

    @pl.when(s == SLABS - 1)
    def _():
        fld[:, 32:48, :] = jnp.zeros((64, 16, 512), F32)
        rat[:, :, 32:48, :] = jnp.zeros((4, 64, 16, 128), F32)

    build_tables(pz, py, px, wzf, wyf, cxf, exf, False)

    for k in range(1, 4):
        shard = near[k]
        to_z(shard, 16, 0, zsend, main_recv).wait_recv()
        for i in range(3):
            to_x(shard, 16, k, i, xsend, main_recv).start()
        halo(shard, k)

    @pl.when(cross)
    def _():
        to_far().wait_recv()
        for i in range(3):
            to_z(v, my_off, i, czsend, cross_recv).start()
        for i in range(3):
            to_x(v, my_off, 0, i, cxsend, cross_recv).start()

    def take(g):
        for k in range(4):
            shard = groups[g][k]
            to_x(shard, 16, k, 0, xsend, main_recv).wait_recv()
            halo(shard, 4 * g + k)

    def z_group(g):
        def one(k, _):
            shard = groups[g][0] - zl + lax.rem(zl + k, GROUP)

            @pl.when(near_lo)
            def _():
                to_up(shard, 0).wait_recv()

            @pl.when(near_hi)
            def _():
                to_dn(shard, 0).wait_recv()

            if g > 0:

                @pl.when(cross)
                def _():
                    to_x(shard, my_off, 0, 0, cxsend, cross_recv).wait_recv()

            z_rows(fld, wzf, thi, tlo, shard * 4, 4)
            return 0

        lax.fori_loop(0, GROUP, one, 0)

    take(1)

    @pl.when(cross)
    def _():
        for k in range(1, 4):
            shard = near[k]
            to_z(shard, my_off, 0, czsend, cross_recv).wait_recv()
            for i in range(3):
                to_x(shard, my_off, k, i, cxsend, cross_recv).start()

    z_group(0)
    take(2)
    z_group(1)
    take(3)
    z_group(2)
    z_group(3)

    x_stage(thi, tlo, cxf, exf, xo)
    load.wait()

    def to_ratio(z, blurred):
        ratio = obs[z] / blurred
        for b in range(4):
            rows = rat.at[b].reshape(3072, 128)
            rows[pl.ds(z + 16, 64, stride=48), :] = ratio[:, 128 * b : 128 * b + 128]

    def up_ratio(c):
        src, dst = (rat.at[:, :, pl.ds(o + 8 * c, 8), :] for o in (16, 0))
        return remote(src, dst, rup_send.at[c], rlo_recv.at[c], (v, s + 1))

    def dn_ratio(c):
        src, dst = (rat.at[:, :, pl.ds(o + 8 * c, 8), :] for o in (16, 32))
        return remote(src, dst, rdn_send.at[c], rhi_recv.at[c], (v, s - 1))

    for c in range(2):
        y_stage(xo, wyf, to_ratio, 8 * c, 8 * c + 8)

        @pl.when(upper)
        def _():
            up_ratio(c).start()

        @pl.when(lower)
        def _():
            dn_ratio(c).start()

    build_tables(pz, py, px, wzb, wyb, cxb, exb, True)

    for c in range(2):

        @pl.when(lower)
        def _():
            up_ratio(c).wait_recv()

        @pl.when(upper)
        def _():
            dn_ratio(c).wait_recv()

    z_stage(rat, wzb, thi, tlo)
    x_stage(thi, tlo, cxb, exb, xo)

    def to_log(z, back):
        logs[z] = jnp.log(back)

    def share_x(c, i):
        src = logs.at[pl.ds(4 * c, 4), pl.ds(pl.multiple_of(xs[i] * 16, 16), 16), :]
        return remote(src, xin.at[i, pl.ds(4 * c, 4)], sx_send.at[c, i], sx_recv.at[c, i], (xpeer[i], s))

    def share_z(c, i):
        j = lax.rem(zl + i + 1, GROUP)
        src = zout.at[j, pl.ds(16 * c, 16), :]
        return remote(src, zin.at[i, pl.ds(16 * c, 16), :], sz_send.at[c, i], sz_recv.at[c, i], (zpeer[i], s))

    def reduce_x(c):
        for i in range(3):
            share_x(c, i).wait_recv()
        for q in range(4):
            z = 4 * c + q
            total = logs[z, pl.ds(pl.multiple_of(x * 16, 16), 16), :]
            for i in range(3):
                total = total + xin[i, z]
            for j in range(4):
                zout[j, 4 * z : 4 * z + 4, :] = total[4 * j : 4 * j + 4]
        for i in range(3):
            share_z(c, i).start()

    def final(c):
        for i in range(3):
            share_z(c, i).wait_recv()
        for q in range(4):
            z = 4 * c + q
            rows = pl.ds(4 * z, 4)
            total = zout[zl, rows, :]
            for i in range(3):
                total = total + zin[i, rows, :]
            out[z] = est[z] * jnp.exp(total)

    for c in range(4):
        y_stage(xo, wyb, to_log, 4 * c, 4 * c + 4)
        for i in range(3):
            share_x(c, i).start()
    for c in range(4):
        reduce_x(c)
    for c in range(4):
        final(c)

    for i in range(3):
        to_z(v, 16, i, zsend, main_recv).wait_send()
        for k in range(4):
            to_x(v, 16, k, i, xsend, main_recv).wait_send()
        for c in range(4):
            share_x(c, i).wait_send()
            share_z(c, i).wait_send()

    @pl.when(cross)
    def _():
        to_far().wait_send()
        for i in range(3):
            to_z(v, my_off, i, czsend, cross_recv).wait_send()
            for k in range(4):
                to_x(v, my_off, k, i, cxsend, cross_recv).wait_send()

    @pl.when(near_hi)
    def _():
        for k in range(16):
            to_up(v, k).wait_send()

    @pl.when(near_lo)
    def _():
        for k in range(16):
            to_dn(v, k).wait_send()

    @pl.when(upper)
    def _():
        for c in range(2):
            up_ratio(c).wait_send()

    @pl.when(lower)
    def _():
        for c in range(2):
            dn_ratio(c).wait_send()


TABLES = [
    pltpu.VMEM((96, 96), BF16),
    pltpu.VMEM((128, 384), BF16),
    pltpu.VMEM((3, 256, 256), BF16),
    pltpu.VMEM((3, 256, 256), BF16),
]
DMA = pltpu.SemaphoreType.DMA
SMEM = pl.BlockSpec(memory_space=pltpu.SMEM)
VM = pl.BlockSpec(memory_space=pltpu.VMEM)
ANY = pl.BlockSpec(memory_space=pl.ANY)


def padded(taps):
    return jnp.pad(taps, ((0, 0), (0, 1)))


def local(estimate, observed, psf_z, psf_y, psf_x):
    pz, py, px = (padded(t[0]) for t in (psf_z, psf_y, psf_x))
    return pl.pallas_call(
        kernel,
        out_shape=jax.ShapeDtypeStruct(estimate.shape, F32),
        in_specs=[SMEM] * 3 + [VM, ANY],
        out_specs=VM,
        scratch_shapes=[
            pltpu.VMEM((64, 48, 512), F32),
            pltpu.VMEM((4, 64, 48, 128), F32),
            pltpu.VMEM((16, 64, 512), F32),
            pltpu.VMEM((64, 48, 512), BF16),
            pltpu.VMEM((64, 48, 512), BF16),
            pltpu.VMEM((4, 3072, 128), F32),
            pltpu.VMEM((16, 64, 512), F32),
            pltpu.VMEM((3, 16, 16, 512), F32),
            pltpu.VMEM((4, 64, 512), F32),
            pltpu.VMEM((3, 64, 512), F32),
        ]
        + TABLES * 2
        + [DMA((1,))]
        + [DMA((16,))] * 4
        + [DMA((3,)), DMA((4, 3)), DMA((16,)), DMA((16,)), DMA((1,)), DMA((3,)), DMA((4, 3))]
        + [DMA((2,))] * 4
        + [DMA((4, 3))] * 4,
        compiler_params=pltpu.CompilerParams(
            collective_id=0, has_side_effects=True, vmem_limit_bytes=60 << 20
        ),
        name="deconvolve",
    )(pz, py, px, estimate, observed[0])


def solution(mesh):
    placed = (
        P("slab", "view", None),
        P("view", "slab", None, None),
        P("view", None, None),
        P("view", None, None),
        P("view", None, None),
    )
    return jax.shard_map(
        local, mesh=mesh, in_specs=placed, out_specs=P("slab", "view", None), check_vma=False
    )
```

```python
import functools

import jax
import jax.numpy as jnp
from jax import lax
from jax.experimental import pallas as pl
from jax.experimental.pallas import tpu as pltpu
from jax.sharding import PartitionSpec as P

RANK = 3
TAPS = 31
HALF = 15
F32, BF16 = jnp.float32, jnp.bfloat16


def split(x):
    hi = x.astype(BF16)
    return hi, (x - hi.astype(F32)).astype(BF16)


def pick(code, count, tap):
    def one(k, acc):
        return jnp.where(code == k, tap(k), acc)

    return lax.fori_loop(0, count, one, jnp.zeros(code.shape, F32))


def iotas(shape):
    return [lax.broadcasted_iota(jnp.int32, shape, d) for d in range(2)]


def build_tables(pz, py, px, wz, wy, cx, ex, back):
    def tap_of(ref):
        return lambda k: ref[k // 32, k % 32]

    row, col = iotas((48, 96))
    p = jnp.where(col < 48, col, col - 48)
    d = (row % 16) - p + 31 if back else p - (row % 16) - 1
    code = jnp.where((d >= 0) & (d < TAPS), (row // 16) * 32 + d, -1)
    hi, lo = split(pick(code, RANK * 32, tap_of(pz)))
    wz[0:48, :] = hi
    wz[48:96, :] = jnp.where(col < 48, lo.astype(F32), 0.0).astype(BF16)

    row, col = iotas((64, 384))
    c = jnp.where(col < 192, col, col - 192)
    d = row - (c % 64) + HALF if back else (c % 64) - row + HALF
    code = jnp.where((d >= 0) & (d < TAPS), (c // 64) * 32 + d, -1)
    hi, lo = split(pick(code, RANK * 32, tap_of(py)))
    wy[0:64, :] = hi
    wy[64:128, :] = jnp.where(col < 192, lo.astype(F32), 0.0).astype(BF16)

    row, col = iotas((128, 128))
    d = col - row + HALF if back else row - col + HALF
    ring = lax.rem(d + 128, 128)
    near = (d >= 0) & (d < TAPS)
    zero = jnp.zeros((128, 128), BF16)
    for r in range(RANK):
        full = pick(ring, TAPS, lambda k: px[r, k])
        for ref, keep in ((cx, near), (ex, jnp.logical_not(near))):
            hi, lo = split(jnp.where(keep, full, 0.0))
            ref[r, 0:128, 0:128] = hi
            ref[r, 0:128, 128:256] = lo
            ref[r, 128:256, 0:128] = hi
            ref[r, 128:256, 128:256] = zero


def dot(a, b):
    return jnp.dot(a, b, preferred_element_type=F32)


def z_stage(src, wz, thi, tlo, unroll=4):
    def one(y, _):
        hi, lo = split(jnp.concatenate([src[b, y] for b in range(4)], axis=1))
        o = dot(wz[...], jnp.concatenate([hi, lo], axis=0))
        hi, lo = split(o[:48] + o[48:])
        thi[y] = hi
        tlo[y] = lo
        return 0

    lax.fori_loop(0, 64, one, 0, unroll=unroll)


def x_stage(thi, tlo, cx, ex, xo, rows=8):
    m = rows * 16
    low = lax.broadcasted_iota(jnp.int32, (m, 128), 1) < 64

    for r in range(RANK):

        def one(c, _):
            ys = pl.ds(c * rows, rows)
            hi = thi[ys, 16 * r : 16 * r + 16, :].reshape(m, 512)
            lo = tlo[ys, 16 * r : 16 * r + 16, :].reshape(m, 512)
            h = [hi[:, 128 * b : 128 * b + 128] for b in range(4)]
            l = [lo[:, 128 * b : 128 * b + 128] for b in range(4)]
            out = []
            for b in range(4):
                o = dot(jnp.concatenate([h[b], l[b]], axis=1), cx[r])
                out.append(o[:, :128] + o[:, 128:])
            for b in range(3):
                ph = jnp.where(low, h[b + 1], h[b])
                pll = jnp.where(low, l[b + 1], l[b])
                o = dot(jnp.concatenate([ph, pll], axis=1), ex[r])
                e = o[:, :128] + o[:, 128:]
                out[b] = out[b] + jnp.where(low, 0.0, e)
                out[b + 1] = out[b + 1] + jnp.where(low, e, 0.0)
            rr = pl.ds(r * 1024 + c * m, m)
            for b in range(4):
                xo[b, rr, :] = out[b]
            return 0

        lax.fori_loop(0, 64 // rows, one, 0)


def y_stage(xo, wy, finish, lo=0, hi=16):
    def one(z, _):
        planes = []
        for r in range(RANK):
            parts = [xo[b, pl.ds(r * 1024 + z, 64, stride=16), :] for b in range(4)]
            planes.append(jnp.concatenate(parts, axis=1))
        h, l = split(jnp.concatenate(planes, axis=0))
        o = dot(wy[...], jnp.concatenate([h, l], axis=0))
        finish(z, o[:64] + o[64:])
        return 0

    lax.fori_loop(lo, hi, one, 0)


SLABS, GROUP = 16, 4
MESH = pl.DeviceIdType.MESH


def remote(src, dst, send, recv, device):
    return pltpu.make_async_remote_copy(
        src_ref=src, dst_ref=dst, send_sem=send, recv_sem=recv, device_id=device, device_id_type=MESH
    )


def z_rows(src, wz, thi, tlo, start, count):
    for i in range(count):
        y = start + i
        hi, lo = split(src[y])
        o = dot(wz[...], jnp.concatenate([hi, lo], axis=0))
        hi, lo = split(o[:48] + o[48:])
        thi[y] = hi
        tlo[y] = lo


def kernel(
    pz, py, px, est, obs_hbm, out,
    fld, rat, relay, obs, thi, tlo, xo, logs, xin, zout, zin,
    wzf, wyf, cxf, exf, wzb, wyb, cxb, exb,
    obs_sem, lo_recv, hi_recv, upsend, dnsend, far_send, far_recv,
    mz_send, mz_recv, mx_send, mx_recv, mc_send, mc_recv,
    cz_send, cz_recv, cx_send, cx_recv, cc_send, cc_recv,
    rup_send, rdn_send, rlo_recv, rhi_recv,
    rel_send, rel_recv, fwd_send, fwd_recv,
    sx_send, sx_recv, sz_send, sz_recv,
):
    v, s = lax.axis_index("view"), lax.axis_index("slab")
    x, zl = lax.div(v, GROUP), lax.rem(v, GROUP)
    zs = [zl, zl + 1 - 2 * lax.rem(zl, 2), lax.rem(zl + 2, GROUP), 3 - zl]
    xs = [x, x + 1 - 2 * lax.rem(x, 2), 3 - x, lax.rem(x + 2, GROUP)]
    zpeer = [x * GROUP + a for a in zs[1:]]
    xpeer = [a * GROUP + zl for a in xs[1:]]
    lower, upper = s > 0, s < SLABS - 1
    cross_lo, cross_hi = s == SLABS // 2, s == SLABS // 2 - 1
    cross = jnp.logical_or(cross_lo, cross_hi)
    near_lo = jnp.logical_and(lower, jnp.logical_not(cross_lo))
    near_hi = jnp.logical_and(upper, jnp.logical_not(cross_hi))
    my_off = pl.multiple_of(jnp.where(cross_lo, 0, 32), 16)
    far_off = pl.multiple_of(jnp.where(cross_lo, 32, 0), 16)
    far_slab = jnp.where(cross_lo, s - 1, s + 1)
    bottom, top = s == 0, s == SLABS - 1
    relays = jnp.logical_or(bottom, top)
    relay_to = jnp.where(bottom, SLABS // 2, SLABS // 2 - 1)
    my_relay = jnp.where(cross_lo, SLABS - 1, 0)

    def block(shard, off):
        return fld.at[pl.ds(shard * 4, 4), pl.ds(off, 16), :]

    for q in range(4):
        fld[v * 4 + q, 16:32, :] = est[:, q, :]

    barrier = pltpu.get_barrier_semaphore()
    for peer in zpeer + xpeer:
        pl.semaphore_signal(barrier, inc=1, device_id=(peer, s), device_id_type=MESH)

    @pl.when(lower)
    def _():
        pl.semaphore_signal(barrier, inc=1, device_id=(v, s - 1), device_id_type=MESH)

    @pl.when(upper)
    def _():
        pl.semaphore_signal(barrier, inc=1, device_id=(v, s + 1), device_id_type=MESH)

    @pl.when(relays)
    def _():
        for peer in (SLABS // 2 - 1, SLABS // 2):
            pl.semaphore_signal(barrier, inc=1, device_id=(v, peer), device_id_type=MESH)

    @pl.when(cross)
    def _():
        for peer in (0, SLABS - 1):
            pl.semaphore_signal(barrier, inc=1, device_id=(v, peer), device_id_type=MESH)

    extra = jnp.where(jnp.logical_or(relays, cross), 2, 0)
    pl.semaphore_wait(barrier, extra + 6 + jnp.where(lower, 1, 0) + jnp.where(upper, 1, 0))

    def shard(j, k):
        return xs[j] * GROUP + zs[k]

    def half(which, off, h):
        return fld.at[pl.ds(which * 4 + 2 * h, 2), pl.ds(off, 16), :]

    main = (16, mz_send, mz_recv, mx_send, mx_recv, mc_send, mc_recv)
    side = (my_off, cz_send, cz_recv, cx_send, cx_recv, cc_send, cc_recv)

    def to_z(stream, i):
        ref = block(v, stream[0])
        return remote(ref, ref, stream[1].at[i], stream[2].at[i], (zpeer[i], s))

    def to_x(stream, i, k, which):
        ref = block(which, stream[0])
        return remote(ref, ref, stream[3].at[i, k], stream[4].at[i, k], (xpeer[i], s))

    def on_x(stream, h, k, which):
        ref = half(which, stream[0], h)
        return remote(ref, ref, stream[5].at[h, k], stream[6].at[h, k], (xpeer[1 - h], s))

    def to_up(which, n):
        return remote(block(which, 16), block(which, 0), upsend.at[n], lo_recv.at[n], (v, s + 1))

    def to_dn(which, n):
        return remote(block(which, 16), block(which, 32), dnsend.at[n], hi_recv.at[n], (v, s - 1))

    def to_far():
        return remote(block(v, 16), block(v, far_off), far_send.at[0], far_recv.at[0], (v, far_slab))

    def halo(stream, j, k):
        if stream is main:

            @pl.when(near_hi)
            def _():
                to_up(shard(j, k), 4 * j + k).start()

            @pl.when(near_lo)
            def _():
                to_dn(shard(j, k), 4 * j + k).start()

    def take_near(stream, k):
        if k > 0:
            to_z(stream, k - 1).wait_recv()
        for i in range(2):
            to_x(stream, i, k, shard(0, k)).start()
        halo(stream, 0, k)

    def take_x(stream, k):
        for i in range(2):
            to_x(stream, i, k, shard(1 + i, k)).wait_recv()
            on_x(stream, i, k, shard(1 + i, k)).start()
            halo(stream, 1 + i, k)

    def take_far(stream, k):
        for h in range(2):
            on_x(stream, h, k, shard(3, k)).wait_recv()
        halo(stream, 3, k)

    @pl.when(cross)
    def _():
        to_far().start()

    for i in range(3):
        to_z(main, i).start()
    take_near(main, 0)
    load = pltpu.make_async_copy(obs_hbm, obs, obs_sem.at[0])
    load.start()

    @pl.when(s == 0)
    def _():
        fld[:, 0:16, :] = jnp.zeros((64, 16, 512), F32)
        rat[:, :, 0:16, :] = jnp.zeros((4, 64, 16, 128), F32)

    @pl.when(s == SLABS - 1)
    def _():
        fld[:, 32:48, :] = jnp.zeros((64, 16, 512), F32)
        rat[:, :, 32:48, :] = jnp.zeros((4, 64, 16, 128), F32)

    build_tables(pz, py, px, wzf, wyf, cxf, exf, False)

    def z_group(k):
        for j in range(4):

            @pl.when(near_lo)
            def _():
                to_up(v, 4 * j + k).wait_recv()

            @pl.when(near_hi)
            def _():
                to_dn(v, 4 * j + k).wait_recv()

        def one(j, _):
            first = lax.rem(xs[0] + j, GROUP) * GROUP + zs[k]
            z_rows(fld, wzf, thi, tlo, first * 4, 4)
            return 0

        lax.fori_loop(0, GROUP, one, 0)

    def crossing(*steps):
        @pl.when(cross)
        def _():
            for step, k in steps:
                step(side, k)

    take_near(main, 1)
    take_x(main, 0)
    take_near(main, 2)
    take_near(main, 3)

    @pl.when(cross)
    def _():
        to_far().wait_recv()
        for i in range(3):
            to_z(side, i).start()
        take_near(side, 0)

    take_far(main, 0)
    take_x(main, 1)
    crossing((take_near, 1), (take_x, 0))
    take_far(main, 1)
    take_x(main, 2)
    crossing((take_near, 2), (take_near, 3), (take_far, 0), (take_x, 1))
    z_group(0)
    take_far(main, 2)
    take_x(main, 3)
    crossing((take_x, 2), (take_far, 1))
    z_group(1)
    take_far(main, 3)
    crossing((take_x, 3), (take_far, 2), (take_far, 3))
    z_group(2)
    z_group(3)

    x_stage(thi, tlo, cxf, exf, xo)
    load.wait()

    def to_ratio(z, blurred):
        ratio = obs[z] / blurred
        for b in range(4):
            rows = rat.at[b].reshape(3072, 128)
            rows[pl.ds(z + 16, 64, stride=48), :] = ratio[:, 128 * b : 128 * b + 128]

    def up_ratio(c):
        src, dst = (rat.at[:, :, pl.ds(o + 8 * c, 8), :] for o in (16, 0))
        return remote(src, dst, rup_send.at[c], rlo_recv.at[c], (v, s + 1))

    def dn_ratio(c):
        src, dst = (rat.at[:, :, pl.ds(o + 8 * c, 8), :] for o in (16, 32))
        return remote(src, dst, rdn_send.at[c], rhi_recv.at[c], (v, s - 1))

    def rows_of(off, c, h):
        return rat.at[:, pl.ds(32 * h, 32), pl.ds(pl.multiple_of(off + 8 * c, 8), 8), :]

    def far_ratio(c):
        src, dst = rows_of(16, c, 0), rows_of(far_off, c, 0)
        return remote(src, dst, far_send.at[1 + c], far_recv.at[1 + c], (v, far_slab))

    def to_relay(c):
        return remote(rows_of(16, c, 1), relay.at[c], rel_send.at[c], rel_recv.at[c], (v, my_relay))

    def from_relay(c):
        dst = rows_of(jnp.where(bottom, 0, 32), c, 1)
        return remote(relay.at[c], dst, fwd_send.at[c], fwd_recv.at[c], (v, relay_to))

    for c in range(2):
        y_stage(xo, wyf, to_ratio, 8 * c, 8 * c + 8)

        @pl.when(cross)
        def _():
            to_relay(c).start()
            far_ratio(c).start()

        @pl.when(near_hi)
        def _():
            up_ratio(c).start()

        @pl.when(near_lo)
        def _():
            dn_ratio(c).start()

    build_tables(pz, py, px, wzb, wyb, cxb, exb, True)

    for c in range(2):

        @pl.when(relays)
        def _():
            to_relay(c).wait_recv()
            from_relay(c).start()

        @pl.when(near_lo)
        def _():
            up_ratio(c).wait_recv()

        @pl.when(near_hi)
        def _():
            dn_ratio(c).wait_recv()

        @pl.when(cross)
        def _():
            far_ratio(c).wait_recv()
            from_relay(c).wait_recv()

    z_stage(rat, wzb, thi, tlo)
    x_stage(thi, tlo, cxb, exb, xo)

    def to_log(z, back):
        logs[z] = jnp.log(back)

    def share_x(c, i):
        src = logs.at[pl.ds(4 * c, 4), pl.ds(pl.multiple_of(xs[i + 1] * 16, 16), 16), :]
        return remote(src, xin.at[i, pl.ds(4 * c, 4)], sx_send.at[c, i], sx_recv.at[c, i], (xpeer[i], s))

    def share_z(c, i):
        j = zs[i + 1]
        src = zout.at[j, pl.ds(16 * c, 16), :]
        return remote(src, zin.at[i, pl.ds(16 * c, 16), :], sz_send.at[c, i], sz_recv.at[c, i], (zpeer[i], s))

    def reduce_x(c):
        for i in range(3):
            share_x(c, i).wait_recv()
        for q in range(4):
            z = 4 * c + q
            total = logs[z, pl.ds(pl.multiple_of(x * 16, 16), 16), :]
            for i in range(3):
                total = total + xin[i, z]
            for j in range(4):
                zout[j, 4 * z : 4 * z + 4, :] = total[4 * j : 4 * j + 4]
        for i in range(3):
            share_z(c, i).start()

    def final(c):
        for i in range(3):
            share_z(c, i).wait_recv()
        for q in range(4):
            z = 4 * c + q
            rows = pl.ds(4 * z, 4)
            total = zout[zl, rows, :]
            for i in range(3):
                total = total + zin[i, rows, :]
            out[z] = est[z] * jnp.exp(total)

    for c in range(4):
        y_stage(xo, wyb, to_log, 4 * c, 4 * c + 4)
        for i in range(3):
            share_x(c, i).start()
    for c in range(4):
        reduce_x(c)
    for c in range(4):
        final(c)

    def drain(stream):
        for i in range(3):
            to_z(stream, i).wait_send()
        for i in range(2):
            for k in range(4):
                to_x(stream, i, k, v).wait_send()
                on_x(stream, i, k, v).wait_send()

    drain(main)
    for i in range(3):
        for c in range(4):
            share_x(c, i).wait_send()
            share_z(c, i).wait_send()

    @pl.when(cross)
    def _():
        drain(side)
        to_far().wait_send()
        for c in range(2):
            far_ratio(c).wait_send()
            to_relay(c).wait_send()

    @pl.when(relays)
    def _():
        for c in range(2):
            from_relay(c).wait_send()

    @pl.when(near_hi)
    def _():
        for k in range(16):
            to_up(v, k).wait_send()
        for c in range(2):
            up_ratio(c).wait_send()

    @pl.when(near_lo)
    def _():
        for k in range(16):
            to_dn(v, k).wait_send()
        for c in range(2):
            dn_ratio(c).wait_send()


TABLES = [
    pltpu.VMEM((96, 96), BF16),
    pltpu.VMEM((128, 384), BF16),
    pltpu.VMEM((3, 256, 256), BF16),
    pltpu.VMEM((3, 256, 256), BF16),
]
DMA = pltpu.SemaphoreType.DMA
SMEM = pl.BlockSpec(memory_space=pltpu.SMEM)
VM = pl.BlockSpec(memory_space=pltpu.VMEM)
ANY = pl.BlockSpec(memory_space=pl.ANY)


def padded(taps):
    return jnp.pad(taps, ((0, 0), (0, 1)))


def local(estimate, observed, psf_z, psf_y, psf_x):
    pz, py, px = (padded(t[0]) for t in (psf_z, psf_y, psf_x))
    return pl.pallas_call(
        kernel,
        out_shape=jax.ShapeDtypeStruct(estimate.shape, F32),
        in_specs=[SMEM] * 3 + [VM, ANY],
        out_specs=VM,
        scratch_shapes=[
            pltpu.VMEM((64, 48, 512), F32),
            pltpu.VMEM((4, 64, 48, 128), F32),
            pltpu.VMEM((2, 4, 32, 8, 128), F32),
            pltpu.VMEM((16, 64, 512), F32),
            pltpu.VMEM((64, 48, 512), BF16),
            pltpu.VMEM((64, 48, 512), BF16),
            pltpu.VMEM((4, 3072, 128), F32),
            pltpu.VMEM((16, 64, 512), F32),
            pltpu.VMEM((3, 16, 16, 512), F32),
            pltpu.VMEM((4, 64, 512), F32),
            pltpu.VMEM((3, 64, 512), F32),
        ]
        + TABLES * 2
        + [DMA((1,))]
        + [DMA((16,))] * 4
        + [DMA((3,))] * 2
        + [DMA((3,)), DMA((3,)), DMA((2, 4)), DMA((2, 4)), DMA((2, 4)), DMA((2, 4))] * 2
        + [DMA((2,))] * 8
        + [DMA((4, 3))] * 4,
        compiler_params=pltpu.CompilerParams(
            collective_id=0, has_side_effects=True, vmem_limit_bytes=60 << 20
        ),
        name="deconvolve",
    )(pz, py, px, estimate, observed[0])


def solution(mesh):
    placed = (
        P("slab", "view", None),
        P("view", "slab", None, None),
        P("view", None, None),
        P("view", None, None),
        P("view", None, None),
    )
    return jax.shard_map(
        local, mesh=mesh, in_specs=placed, out_specs=P("slab", "view", None), check_vma=False
    )
```

```python
import functools

import jax
import jax.numpy as jnp
from jax import lax
from jax.experimental import pallas as pl
from jax.experimental.pallas import tpu as pltpu
from jax.sharding import PartitionSpec as P

RANK = 3
TAPS = 31
HALF = 15
F32, BF16 = jnp.float32, jnp.bfloat16


def split(x):
    hi = x.astype(BF16)
    return hi, (x - hi.astype(F32)).astype(BF16)


def pick(code, count, tap):
    def one(k, acc):
        return jnp.where(code == k, tap(k), acc)

    return lax.fori_loop(0, count, one, jnp.zeros(code.shape, F32))


def iotas(shape):
    return [lax.broadcasted_iota(jnp.int32, shape, d) for d in range(2)]


def build_tables(pz, py, px, wz, wy, cx, ex, back):
    def tap_of(ref):
        return lambda k: ref[0, k // TAPS, k % TAPS]

    row, col = iotas((48, 96))
    p = jnp.where(col < 48, col, col - 48)
    d = (row % 16) - p + 31 if back else p - (row % 16) - 1
    code = jnp.where((d >= 0) & (d < TAPS), (row // 16) * TAPS + d, -1)
    hi, lo = split(pick(code, RANK * TAPS, tap_of(pz)))
    wz[0:48, :] = hi
    wz[48:96, :] = jnp.where(col < 48, lo.astype(F32), 0.0).astype(BF16)

    row, col = iotas((64, 384))
    c = jnp.where(col < 192, col, col - 192)
    d = row - (c % 64) + HALF if back else (c % 64) - row + HALF
    code = jnp.where((d >= 0) & (d < TAPS), (c // 64) * TAPS + d, -1)
    hi, lo = split(pick(code, RANK * TAPS, tap_of(py)))
    wy[0:64, :] = hi
    wy[64:128, :] = jnp.where(col < 192, lo.astype(F32), 0.0).astype(BF16)

    row, col = iotas((128, 128))
    d = col - row + HALF if back else row - col + HALF
    ring = lax.rem(d + 128, 128)
    near = (d >= 0) & (d < TAPS)
    zero = jnp.zeros((128, 128), BF16)
    for r in range(RANK):
        full = pick(ring, TAPS, lambda k: px[0, r, k])
        for ref, keep in ((cx, near), (ex, jnp.logical_not(near))):
            hi, lo = split(jnp.where(keep, full, 0.0))
            ref[r, 0:128, 0:128] = hi
            ref[r, 0:128, 128:256] = lo
            ref[r, 128:256, 0:128] = hi
            ref[r, 128:256, 128:256] = zero


def dot(a, b):
    return jnp.dot(a, b, preferred_element_type=F32)


def z_rows(load, wz, thi, tlo, start, count):
    for i in range(0, count, 2):
        pair = []
        for y in (start + i, start + i + 1):
            hi, lo = split(load(y))
            o = dot(wz[...], jnp.concatenate([hi, lo], axis=0))
            pair.append(o[:48] + o[48:])
        rows = pl.ds(pl.multiple_of((start + i) * 8, 16), 16)
        for h in range(2):
            for r in range(RANK):
                top = 16 * r + 8 * h
                hi, lo = split(jnp.concatenate([p[top : top + 8] for p in pair], axis=0))
                thi[h, r, rows, :] = hi
                tlo[h, r, rows, :] = lo


def x_stage(thi, tlo, cx, ex, xo, h, m=512):
    low = lax.broadcasted_iota(jnp.int32, (m, 128), 1) < 64

    for r in range(RANK):

        def one(c, _):
            rows = pl.ds(pl.multiple_of(c * m, m), m)
            dest = pl.ds(pl.multiple_of(r * 512 + c * m, m), m)

            def lanes(ref, b):
                return ref[h, r, rows, 128 * b : 128 * b + 128]

            before = jnp.zeros((m, 128), F32)
            for b in range(4):
                hi, lo = lanes(thi, b), lanes(tlo, b)
                o = dot(jnp.concatenate([hi, lo], axis=1), cx[r])
                after = jnp.zeros((m, 128), F32)
                if b < 3:
                    hi = jnp.where(low, lanes(thi, b + 1), hi)
                    lo = jnp.where(low, lanes(tlo, b + 1), lo)
                    e = dot(jnp.concatenate([hi, lo], axis=1), ex[r])
                    after = e[:, :128] + e[:, 128:]
                xo[h, b, dest, :] = o[:, :128] + o[:, 128:] + jnp.where(low, before, after)
                before = after
            return 0

        lax.fori_loop(0, 512 // m, one, 0, unroll=1)


def y_stage(xo, wy, finish, h, lo=0, hi=8):
    def one(z, _):
        planes = []
        for r in range(RANK):
            parts = [xo[h, b, pl.ds(r * 512 + z, 64, stride=8), :] for b in range(4)]
            planes.append(jnp.concatenate(parts, axis=1))
        a, l = split(jnp.concatenate(planes, axis=0))
        o = dot(wy[...], jnp.concatenate([a, l], axis=0))
        finish(8 * h + z, o[:64] + o[64:])
        return 0

    lax.fori_loop(lo, hi, one, 0, unroll=4)


SLABS, GROUP = 16, 4
DIRECT, PIECE = 36, 14
MESH = pl.DeviceIdType.MESH


def remote(src, dst, send, recv, device):
    return pltpu.make_async_remote_copy(
        src_ref=src, dst_ref=dst, send_sem=send, recv_sem=recv, device_id=device, device_id_type=MESH
    )


def kernel(
    pz, py, px, est, obs_hbm, out,
    fld, rat, relay, obs, thi, tlo, xo, logs, pin, xin, zout, zin,
    wzf, wyf, cxf, exf, wzb, wyb, cxb, exb,
    obs_sem, lo_recv, hi_recv, upsend, dnsend, far_send, far_recv,
    mz_send, mz_recv, mx_send, mx_recv, mc_send, mc_recv,
    cz_send, cz_recv, cx_send, cx_recv, cc_send, cc_recv,
    rup_send, rdn_send, rlo_recv, rhi_recv,
    rel_send, rel_recv, fwd_send, fwd_recv,
    sp_send, sp_recv, sx_send, sx_recv, sz_send, sz_recv,
):
    v, s = lax.axis_index("view"), lax.axis_index("slab")
    x, zl = lax.div(v, GROUP), lax.rem(v, GROUP)
    zs = [zl, zl + 1 - 2 * lax.rem(zl, 2), lax.rem(zl + 2, GROUP), 3 - zl]
    xs = [x, x + 1 - 2 * lax.rem(x, 2), 3 - x, lax.rem(x + 2, GROUP)]
    zpeer = [x * GROUP + a for a in zs[1:]]
    xpeer = [a * GROUP + zl for a in xs[1:]]
    lower, upper = s > 0, s < SLABS - 1
    cross_lo, cross_hi = s == SLABS // 2, s == SLABS // 2 - 1
    cross = jnp.logical_or(cross_lo, cross_hi)
    near_lo = jnp.logical_and(lower, jnp.logical_not(cross_lo))
    near_hi = jnp.logical_and(upper, jnp.logical_not(cross_hi))
    my_off = pl.multiple_of(jnp.where(cross_lo, 0, 32), 16)
    far_off = pl.multiple_of(jnp.where(cross_lo, 32, 0), 16)
    far_slab = jnp.where(cross_lo, s - 1, s + 1)
    bottom, top = s == 0, s == SLABS - 1
    relays = jnp.logical_or(bottom, top)
    relay_to = jnp.where(bottom, SLABS // 2, SLABS // 2 - 1)
    my_relay = jnp.where(cross_lo, SLABS - 1, 0)

    def block(shard, off):
        return fld.at[pl.ds(shard * 4, 4), pl.ds(off, 16), :]

    for q in range(4):
        fld[v * 4 + q, 16:32, :] = est[:, q, :]

    barrier = pltpu.get_barrier_semaphore()
    for peer in zpeer + xpeer:
        pl.semaphore_signal(barrier, inc=1, device_id=(peer, s), device_id_type=MESH)

    @pl.when(lower)
    def _():
        pl.semaphore_signal(barrier, inc=1, device_id=(v, s - 1), device_id_type=MESH)

    @pl.when(upper)
    def _():
        pl.semaphore_signal(barrier, inc=1, device_id=(v, s + 1), device_id_type=MESH)

    @pl.when(relays)
    def _():
        for peer in (SLABS // 2 - 1, SLABS // 2):
            pl.semaphore_signal(barrier, inc=1, device_id=(v, peer), device_id_type=MESH)

    @pl.when(cross)
    def _():
        for peer in (0, SLABS - 1):
            pl.semaphore_signal(barrier, inc=1, device_id=(v, peer), device_id_type=MESH)

    extra = jnp.where(jnp.logical_or(relays, cross), 2, 0)
    pl.semaphore_wait(barrier, extra + 6 + jnp.where(lower, 1, 0) + jnp.where(upper, 1, 0))

    def shard(j, k):
        return xs[j] * GROUP + zs[k]

    def half(which, off, h):
        return fld.at[pl.ds(which * 4 + 2 * h, 2), pl.ds(off, 16), :]

    main = (16, mz_send, mz_recv, mx_send, mx_recv, mc_send, mc_recv)
    side = (my_off, cz_send, cz_recv, cx_send, cx_recv, cc_send, cc_recv)

    def to_z(stream, i):
        ref = block(v, stream[0])
        return remote(ref, ref, stream[1].at[i], stream[2].at[i], (zpeer[i], s))

    def to_x(stream, i, k, which):
        ref = block(which, stream[0])
        return remote(ref, ref, stream[3].at[i, k], stream[4].at[i, k], (xpeer[i], s))

    def on_x(stream, h, k, which):
        ref = half(which, stream[0], h)
        return remote(ref, ref, stream[5].at[h, k], stream[6].at[h, k], (xpeer[1 - h], s))

    def to_up(which, n):
        return remote(block(which, 16), block(which, 0), upsend.at[n], lo_recv.at[n], (v, s + 1))

    def to_dn(which, n):
        return remote(block(which, 16), block(which, 32), dnsend.at[n], hi_recv.at[n], (v, s - 1))

    def to_far():
        return remote(block(v, 16), block(v, far_off), far_send.at[0], far_recv.at[0], (v, far_slab))

    def halo(stream, j, k):
        if stream is main:

            @pl.when(near_hi)
            def _():
                to_up(shard(j, k), 4 * j + k).start()

            @pl.when(near_lo)
            def _():
                to_dn(shard(j, k), 4 * j + k).start()

    def take_near(stream, k):
        if k > 0:
            to_z(stream, k - 1).wait_recv()
        for i in range(2):
            to_x(stream, i, k, shard(0, k)).start()
        halo(stream, 0, k)

    def take_x(stream, k):
        for i in range(2):
            to_x(stream, i, k, shard(1 + i, k)).wait_recv()
            on_x(stream, i, k, shard(1 + i, k)).start()
            halo(stream, 1 + i, k)

    def take_far(stream, k):
        for h in range(2):
            on_x(stream, h, k, shard(3, k)).wait_recv()
        halo(stream, 3, k)

    @pl.when(cross)
    def _():
        to_far().start()

    for i in range(3):
        to_z(main, i).start()
    take_near(main, 0)
    load = pltpu.make_async_copy(obs_hbm, obs, obs_sem.at[0])
    load.start()

    @pl.when(s == 0)
    def _():
        fld[:, 0:16, :] = jnp.zeros((64, 16, 512), F32)
        rat[:, :, 0:16, :] = jnp.zeros((4, 64, 16, 128), F32)

    @pl.when(s == SLABS - 1)
    def _():
        fld[:, 32:48, :] = jnp.zeros((64, 16, 512), F32)
        rat[:, :, 32:48, :] = jnp.zeros((4, 64, 16, 128), F32)

    build_tables(pz, py, px, wzf, wyf, cxf, exf, False)

    def z_group(k):
        for j in range(4):

            @pl.when(near_lo)
            def _():
                to_up(v, 4 * j + k).wait_recv()

            @pl.when(near_hi)
            def _():
                to_dn(v, 4 * j + k).wait_recv()

        def one(j, _):
            first = lax.rem(xs[0] + j, GROUP) * GROUP + zs[k]
            z_rows(lambda y: fld[y], wzf, thi, tlo, first * 4, 4)
            return 0

        lax.fori_loop(0, GROUP, one, 0)

    def crossing(*steps):
        @pl.when(cross)
        def _():
            for step, k in steps:
                step(side, k)

    take_near(main, 1)
    take_x(main, 0)
    take_near(main, 2)
    take_near(main, 3)

    @pl.when(cross)
    def _():
        to_far().wait_recv()
        for i in range(3):
            to_z(side, i).start()
        take_near(side, 0)

    take_far(main, 0)
    take_x(main, 1)
    crossing((take_near, 1), (take_x, 0))
    take_far(main, 1)
    take_x(main, 2)
    crossing((take_near, 2), (take_near, 3), (take_far, 0), (take_x, 1))
    z_group(0)
    take_far(main, 2)
    take_x(main, 3)
    crossing((take_x, 2), (take_far, 1))
    z_group(1)
    take_far(main, 3)
    crossing((take_x, 3), (take_far, 2), (take_far, 3))
    z_group(2)
    z_group(3)

    load.wait()

    def to_ratio(z, blurred):
        ratio = obs[z] / blurred
        for b in range(4):
            rows = rat.at[b].reshape(3072, 128)
            rows[pl.ds(z + 16, 64, stride=48), :] = ratio[:, 128 * b : 128 * b + 128]

    def up_ratio(c):
        src, dst = (rat.at[:, :, pl.ds(o + 8 * c, 8), :] for o in (16, 0))
        return remote(src, dst, rup_send.at[c], rlo_recv.at[c], (v, s + 1))

    def dn_ratio(c):
        src, dst = (rat.at[:, :, pl.ds(o + 8 * c, 8), :] for o in (16, 32))
        return remote(src, dst, rdn_send.at[c], rhi_recv.at[c], (v, s - 1))

    def rows_of(off, c, first, count):
        return rat.at[:, pl.ds(first, count), pl.ds(pl.multiple_of(off + 8 * c, 8), 8), :]

    def far_ratio(c):
        src, dst = rows_of(16, c, 0, DIRECT), rows_of(far_off, c, 0, DIRECT)
        return remote(src, dst, far_send.at[1 + c], far_recv.at[1 + c], (v, far_slab))

    def to_relay(c, p):
        src = rows_of(16, c, DIRECT + PIECE * p, PIECE)
        return remote(src, relay.at[c, p], rel_send.at[c, p], rel_recv.at[c, p], (v, my_relay))

    def from_relay(c, p):
        dst = rows_of(jnp.where(bottom, 0, 32), c, DIRECT + PIECE * p, PIECE)
        return remote(relay.at[c, p], dst, fwd_send.at[c, p], fwd_recv.at[c, p], (v, relay_to))

    for c in range(2):
        x_stage(thi, tlo, cxf, exf, xo, c)
        y_stage(xo, wyf, to_ratio, c)

        @pl.when(cross)
        def _():
            to_relay(c, 0).start()
            to_relay(c, 1).start()
            far_ratio(c).start()

        @pl.when(near_hi)
        def _():
            up_ratio(c).start()

        @pl.when(near_lo)
        def _():
            dn_ratio(c).start()

    build_tables(pz, py, px, wzb, wyb, cxb, exb, True)

    for c in range(2):

        @pl.when(relays)
        def _():
            for p in range(2):
                to_relay(c, p).wait_recv()
                from_relay(c, p).start()

        @pl.when(near_lo)
        def _():
            up_ratio(c).wait_recv()

        @pl.when(near_hi)
        def _():
            dn_ratio(c).wait_recv()

        @pl.when(cross)
        def _():
            far_ratio(c).wait_recv()
            for p in range(2):
                from_relay(c, p).wait_recv()

    def ratio_rows(y):
        return jnp.concatenate([rat[b, y] for b in range(4)], axis=1)

    def z_back(n, _):
        z_rows(ratio_rows, wzb, thi, tlo, n * 16, 16)
        return 0

    lax.fori_loop(0, 64 // 16, z_back, 0)

    def to_log(z, back):
        logs[z] = jnp.log(back)

    def x_rows(j, c, first, count):
        start = pl.multiple_of(xs[j] * 16 + first, 8)
        return logs.at[pl.ds(4 * c, 4), pl.ds(start, count), :]

    def share_far(c, i):
        dst = pin.at[i, pl.ds(4 * c, 4)]
        return remote(x_rows(3, c, 8 - 8 * i, 8), dst, sp_send.at[c, i], sp_recv.at[c, i], (xpeer[i], s))

    def share_x(c, i):
        dst = xin.at[i, pl.ds(4 * c, 4)]
        return remote(x_rows(1 + i, c, 0, 16), dst, sx_send.at[c, i], sx_recv.at[c, i], (xpeer[i], s))

    def share_z(c, i):
        j = zs[i + 1]
        src = zout.at[j, pl.ds(16 * c, 16), :]
        return remote(src, zin.at[i, pl.ds(16 * c, 16), :], sz_send.at[c, i], sz_recv.at[c, i], (zpeer[i], s))

    def send_far(c):
        for i in range(2):
            share_far(c, i).start()

    def send_near(c):
        for i in range(2):
            share_far(c, i).wait_recv()
            j, first = 2 - i, 8 - 8 * i
            ref = x_rows(j, c, first, 8)
            ref[...] = ref[...] + pin[i, 4 * c : 4 * c + 4]
        for i in range(2):
            share_x(c, i).start()

    def reduce_x(c):
        for i in range(2):
            share_x(c, i).wait_recv()
        for q in range(4):
            z = 4 * c + q
            total = logs[z, pl.ds(pl.multiple_of(x * 16, 16), 16), :]
            for i in range(2):
                total = total + xin[i, z]
            for j in range(4):
                zout[j, 4 * z : 4 * z + 4, :] = total[4 * j : 4 * j + 4]
        for i in range(3):
            share_z(c, i).start()

    def final(c):
        for i in range(3):
            share_z(c, i).wait_recv()
        for q in range(4):
            z = 4 * c + q
            rows = pl.ds(4 * z, 4)
            total = zout[zl, rows, :]
            for i in range(3):
                total = total + zin[i, rows, :]
            out[z] = total

    x_stage(thi, tlo, cxb, exb, xo, 0)
    y_stage(xo, wyb, to_log, 0, 0, 4)
    send_far(0)
    y_stage(xo, wyb, to_log, 0, 4, 8)
    send_far(1)
    x_stage(thi, tlo, cxb, exb, xo, 1)
    send_near(0)
    y_stage(xo, wyb, to_log, 1, 0, 4)
    send_far(2)
    send_near(1)
    y_stage(xo, wyb, to_log, 1, 4, 8)
    send_far(3)
    send_near(2)
    reduce_x(0)
    send_near(3)
    for c in range(1, 4):
        reduce_x(c)
    for c in range(4):
        final(c)

    def drain(stream):
        for i in range(3):
            to_z(stream, i).wait_send()
        for i in range(2):
            for k in range(4):
                to_x(stream, i, k, v).wait_send()
                on_x(stream, i, k, v).wait_send()

    drain(main)
    for c in range(4):
        for i in range(2):
            share_far(c, i).wait_send()
            share_x(c, i).wait_send()
        for i in range(3):
            share_z(c, i).wait_send()

    @pl.when(cross)
    def _():
        drain(side)
        to_far().wait_send()
        for c in range(2):
            far_ratio(c).wait_send()
            to_relay(c, 0).wait_send()
            to_relay(c, 1).wait_send()

    @pl.when(relays)
    def _():
        for c in range(2):
            from_relay(c, 0).wait_send()
            from_relay(c, 1).wait_send()

    @pl.when(near_hi)
    def _():
        for k in range(16):
            to_up(v, k).wait_send()
        for c in range(2):
            up_ratio(c).wait_send()

    @pl.when(near_lo)
    def _():
        for k in range(16):
            to_dn(v, k).wait_send()
        for c in range(2):
            dn_ratio(c).wait_send()


TABLES = [
    pltpu.VMEM((96, 96), BF16),
    pltpu.VMEM((128, 384), BF16),
    pltpu.VMEM((3, 256, 256), BF16),
    pltpu.VMEM((3, 256, 256), BF16),
]
DMA = pltpu.SemaphoreType.DMA
SMEM = pl.BlockSpec(memory_space=pltpu.SMEM)
VM = pl.BlockSpec(memory_space=pltpu.VMEM)
ANY = pl.BlockSpec(memory_space=pl.ANY)


def local(estimate, observed, psf_z, psf_y, psf_x):
    share = pl.pallas_call(
        kernel,
        out_shape=jax.ShapeDtypeStruct(estimate.shape, F32),
        in_specs=[SMEM] * 3 + [VM, ANY],
        out_specs=VM,
        scratch_shapes=[
            pltpu.VMEM((64, 48, 512), F32),
            pltpu.VMEM((4, 64, 48, 128), F32),
            pltpu.VMEM((2, 2, 4, PIECE, 8, 128), F32),
            pltpu.VMEM((16, 64, 512), F32),
            pltpu.VMEM((2, 3, 512, 512), BF16),
            pltpu.VMEM((2, 3, 512, 512), BF16),
            pltpu.VMEM((2, 4, 1536, 128), F32),
            pltpu.VMEM((16, 64, 512), F32),
            pltpu.VMEM((2, 16, 8, 512), F32),
            pltpu.VMEM((2, 16, 16, 512), F32),
            pltpu.VMEM((4, 64, 512), F32),
            pltpu.VMEM((3, 64, 512), F32),
        ]
        + TABLES * 2
        + [DMA((1,))]
        + [DMA((16,))] * 4
        + [DMA((3,))] * 2
        + [DMA((3,)), DMA((3,)), DMA((2, 4)), DMA((2, 4)), DMA((2, 4)), DMA((2, 4))] * 2
        + [DMA((2,))] * 4
        + [DMA((2, 2))] * 4
        + [DMA((4, 2))] * 4
        + [DMA((4, 3))] * 2,
        compiler_params=pltpu.CompilerParams(
            collective_id=0, has_side_effects=True, vmem_limit_bytes=60 << 20
        ),
        name="deconvolve",
    )(psf_z, psf_y, psf_x, estimate, observed[0])
    return estimate * jnp.exp(share)


def solution(mesh):
    placed = (
        P("slab", "view", None),
        P("view", "slab", None, None),
        P("view", None, None),
        P("view", None, None),
        P("view", None, None),
    )
    return jax.shard_map(
        local, mesh=mesh, in_specs=placed, out_specs=P("slab", "view", None), check_vma=False
    )
```

```python
import functools

import jax
import jax.numpy as jnp
from jax import lax
from jax.experimental import pallas as pl
from jax.experimental.pallas import tpu as pltpu
from jax.sharding import PartitionSpec as P

RANK = 3
TAPS = 31
HALF = 15
F32, BF16 = jnp.float32, jnp.bfloat16


def split(x):
    hi = x.astype(BF16)
    return hi, (x - hi.astype(F32)).astype(BF16)


def pick(code, count, tap):
    def one(k, acc):
        return jnp.where(code == k, tap(k), acc)

    return lax.fori_loop(0, count, one, jnp.zeros(code.shape, F32))


def iotas(shape):
    return [lax.broadcasted_iota(jnp.int32, shape, d) for d in range(2)]


def build_tables(pz, py, px, wz, wy, cx, ex, back):
    def tap_of(ref):
        return lambda k: ref[k // TAPS, 0, k % TAPS]

    row, col = iotas((48, 96))
    p = jnp.where(col < 48, col, col - 48)
    d = (row % 16) - p + 31 if back else p - (row % 16) - 1
    code = jnp.where((d >= 0) & (d < TAPS), (row // 16) * TAPS + d, -1)
    hi, lo = split(pick(code, RANK * TAPS, tap_of(pz)))
    wz[0:48, :] = hi
    wz[48:96, :] = jnp.where(col < 48, lo.astype(F32), 0.0).astype(BF16)

    row, col = iotas((64, 384))
    c = jnp.where(col < 192, col, col - 192)
    d = row - (c % 64) + HALF if back else (c % 64) - row + HALF
    code = jnp.where((d >= 0) & (d < TAPS), (c // 64) * TAPS + d, -1)
    hi, lo = split(pick(code, RANK * TAPS, tap_of(py)))
    wy[0:64, :] = hi
    wy[64:128, :] = jnp.where(col < 192, lo.astype(F32), 0.0).astype(BF16)

    row, col = iotas((128, 128))
    d = col - row + HALF if back else row - col + HALF
    ring = lax.rem(d + 128, 128)
    near = (d >= 0) & (d < TAPS)
    zero = jnp.zeros((128, 128), BF16)
    for r in range(RANK):
        full = pick(ring, TAPS, lambda k: px[r, 0, k])
        for ref, keep in ((cx, near), (ex, jnp.logical_not(near))):
            hi, lo = split(jnp.where(keep, full, 0.0))
            ref[r, 0:128, 0:128] = hi
            ref[r, 0:128, 128:256] = lo
            ref[r, 128:256, 0:128] = hi
            ref[r, 128:256, 128:256] = zero


def dot(a, b):
    return jnp.dot(a, b, preferred_element_type=F32)


def z_rows(load, wz, thi, tlo, start, count):
    for i in range(0, count, 2):
        pair = []
        for y in (start + i, start + i + 1):
            hi, lo = split(load(y))
            o = dot(wz[...], jnp.concatenate([hi, lo], axis=0))
            pair.append(o[:48] + o[48:])
        rows = pl.ds(pl.multiple_of((start + i) * 8, 16), 16)
        for h in range(2):
            for r in range(RANK):
                top = 16 * r + 8 * h
                hi, lo = split(jnp.concatenate([p[top : top + 8] for p in pair], axis=0))
                thi[h, r, rows, :] = hi
                tlo[h, r, rows, :] = lo


def x_stage(thi, tlo, cx, ex, xo, h, m=512):
    low = lax.broadcasted_iota(jnp.int32, (m, 128), 1) < 64

    for r in range(RANK):

        def one(c, _):
            rows = pl.ds(pl.multiple_of(c * m, m), m)
            dest = pl.ds(pl.multiple_of(r * 512 + c * m, m), m)

            def lanes(ref, b):
                return ref[h, r, rows, 128 * b : 128 * b + 128]

            before = jnp.zeros((m, 128), F32)
            for b in range(4):
                hi, lo = lanes(thi, b), lanes(tlo, b)
                o = dot(jnp.concatenate([hi, lo], axis=1), cx[r])
                after = jnp.zeros((m, 128), F32)
                if b < 3:
                    hi = jnp.where(low, lanes(thi, b + 1), hi)
                    lo = jnp.where(low, lanes(tlo, b + 1), lo)
                    e = dot(jnp.concatenate([hi, lo], axis=1), ex[r])
                    after = e[:, :128] + e[:, 128:]
                xo[h, b, dest, :] = o[:, :128] + o[:, 128:] + jnp.where(low, before, after)
                before = after
            return 0

        lax.fori_loop(0, 512 // m, one, 0, unroll=1)


def y_stage(xo, wy, finish, h, lo=0, hi=8):
    def one(z, _):
        planes = []
        for r in range(RANK):
            parts = [xo[h, b, pl.ds(r * 512 + z, 64, stride=8), :] for b in range(4)]
            planes.append(jnp.concatenate(parts, axis=1))
        a, l = split(jnp.concatenate(planes, axis=0))
        o = dot(wy[...], jnp.concatenate([a, l], axis=0))
        finish(8 * h + z, o[:64] + o[64:])
        return 0

    lax.fori_loop(lo, hi, one, 0, unroll=4)


SLABS, GROUP = 16, 4
DIRECT, PIECE = 34, 15
MESH = pl.DeviceIdType.MESH


def remote(src, dst, send, recv, device):
    return pltpu.make_async_remote_copy(
        src_ref=src, dst_ref=dst, send_sem=send, recv_sem=recv, device_id=device, device_id_type=MESH
    )


def kernel(
    pz, py, px, est, obs_hbm, out,
    fld, rat, relay, obs, thi, tlo, xo, logs, pin, xin, zout, zin,
    wzf, wyf, cxf, exf, wzb, wyb, cxb, exb,
    obs_sem, lo_recv, hi_recv, upsend, dnsend, far_send, far_recv,
    mz_send, mz_recv, mx_send, mx_recv, mc_send, mc_recv,
    cz_send, cz_recv, cx_send, cx_recv, cc_send, cc_recv,
    rup_send, rdn_send, rlo_recv, rhi_recv,
    rel_send, rel_recv, fwd_send, fwd_recv,
    sp_send, sp_recv, sx_send, sx_recv, sz_send, sz_recv,
):
    v, s = lax.axis_index("view"), lax.axis_index("slab")
    x, zl = lax.div(v, GROUP), lax.rem(v, GROUP)
    zs = [zl, zl + 1 - 2 * lax.rem(zl, 2), lax.rem(zl + 2, GROUP), 3 - zl]
    xs = [x, x + 1 - 2 * lax.rem(x, 2), 3 - x, lax.rem(x + 2, GROUP)]
    zpeer = [x * GROUP + a for a in zs[1:]]
    xpeer = [a * GROUP + zl for a in xs[1:]]
    lower, upper = s > 0, s < SLABS - 1
    cross_lo, cross_hi = s == SLABS // 2, s == SLABS // 2 - 1
    cross = jnp.logical_or(cross_lo, cross_hi)
    near_lo = jnp.logical_and(lower, jnp.logical_not(cross_lo))
    near_hi = jnp.logical_and(upper, jnp.logical_not(cross_hi))
    my_off = pl.multiple_of(jnp.where(cross_lo, 0, 32), 16)
    far_off = pl.multiple_of(jnp.where(cross_lo, 32, 0), 16)
    far_slab = jnp.where(cross_lo, s - 1, s + 1)
    bottom, top = s == 0, s == SLABS - 1
    relays = jnp.logical_or(bottom, top)
    relay_to = jnp.where(bottom, SLABS // 2, SLABS // 2 - 1)
    my_relay = jnp.where(cross_lo, SLABS - 1, 0)

    def block(shard, off):
        return fld.at[pl.ds(shard * 4, 4), pl.ds(off, 16), :]

    for q in range(4):
        fld[v * 4 + q, 16:32, :] = est[:, q, :]

    barrier = pltpu.get_barrier_semaphore()
    for peer in zpeer + xpeer:
        pl.semaphore_signal(barrier, inc=1, device_id=(peer, s), device_id_type=MESH)

    @pl.when(lower)
    def _():
        pl.semaphore_signal(barrier, inc=1, device_id=(v, s - 1), device_id_type=MESH)

    @pl.when(upper)
    def _():
        pl.semaphore_signal(barrier, inc=1, device_id=(v, s + 1), device_id_type=MESH)

    @pl.when(relays)
    def _():
        for peer in (SLABS // 2 - 1, SLABS // 2):
            pl.semaphore_signal(barrier, inc=1, device_id=(v, peer), device_id_type=MESH)

    @pl.when(cross)
    def _():
        for peer in (0, SLABS - 1):
            pl.semaphore_signal(barrier, inc=1, device_id=(v, peer), device_id_type=MESH)

    extra = jnp.where(jnp.logical_or(relays, cross), 2, 0)
    pl.semaphore_wait(barrier, extra + 6 + jnp.where(lower, 1, 0) + jnp.where(upper, 1, 0))

    def shard(j, k):
        return xs[j] * GROUP + zs[k]

    def half(which, off, h):
        return fld.at[pl.ds(which * 4 + 2 * h, 2), pl.ds(off, 16), :]

    main = (16, mz_send, mz_recv, mx_send, mx_recv, mc_send, mc_recv)
    side = (my_off, cz_send, cz_recv, cx_send, cx_recv, cc_send, cc_recv)

    def to_z(stream, i):
        ref = block(v, stream[0])
        return remote(ref, ref, stream[1].at[i], stream[2].at[i], (zpeer[i], s))

    def to_x(stream, i, k, which):
        ref = block(which, stream[0])
        return remote(ref, ref, stream[3].at[i, k], stream[4].at[i, k], (xpeer[i], s))

    def on_x(stream, h, k, which):
        ref = half(which, stream[0], h)
        return remote(ref, ref, stream[5].at[h, k], stream[6].at[h, k], (xpeer[1 - h], s))

    def to_up(which, n):
        return remote(block(which, 16), block(which, 0), upsend.at[n], lo_recv.at[n], (v, s + 1))

    def to_dn(which, n):
        return remote(block(which, 16), block(which, 32), dnsend.at[n], hi_recv.at[n], (v, s - 1))

    def to_far():
        return remote(block(v, 16), block(v, far_off), far_send.at[0], far_recv.at[0], (v, far_slab))

    def halo(stream, j, k):
        if stream is main:

            @pl.when(near_hi)
            def _():
                to_up(shard(j, k), 4 * j + k).start()

            @pl.when(near_lo)
            def _():
                to_dn(shard(j, k), 4 * j + k).start()

    def take_near(stream, k):
        if k > 0:
            to_z(stream, k - 1).wait_recv()
        for i in range(2):
            to_x(stream, i, k, shard(0, k)).start()
        halo(stream, 0, k)

    def take_x(stream, k):
        for i in range(2):
            to_x(stream, i, k, shard(1 + i, k)).wait_recv()
            on_x(stream, i, k, shard(1 + i, k)).start()
            halo(stream, 1 + i, k)

    def take_far(stream, k):
        for h in range(2):
            on_x(stream, h, k, shard(3, k)).wait_recv()
        halo(stream, 3, k)

    @pl.when(cross)
    def _():
        to_far().start()

    for i in range(3):
        to_z(main, i).start()
    take_near(main, 0)
    load = pltpu.make_async_copy(obs_hbm, obs, obs_sem.at[0])
    load.start()

    @pl.when(s == 0)
    def _():
        fld[:, 0:16, :] = jnp.zeros((64, 16, 512), F32)
        rat[:, :, 0:16, :] = jnp.zeros((4, 64, 16, 128), F32)

    @pl.when(s == SLABS - 1)
    def _():
        fld[:, 32:48, :] = jnp.zeros((64, 16, 512), F32)
        rat[:, :, 32:48, :] = jnp.zeros((4, 64, 16, 128), F32)

    build_tables(pz, py, px, wzf, wyf, cxf, exf, False)

    def z_group(k):
        for j in range(4):

            @pl.when(near_lo)
            def _():
                to_up(v, 4 * j + k).wait_recv()

            @pl.when(near_hi)
            def _():
                to_dn(v, 4 * j + k).wait_recv()

        def one(j, _):
            first = lax.rem(xs[0] + j, GROUP) * GROUP + zs[k]
            z_rows(lambda y: fld[y], wzf, thi, tlo, first * 4, 4)
            return 0

        lax.fori_loop(0, GROUP, one, 0)

    def crossing(*steps):
        @pl.when(cross)
        def _():
            for step, k in steps:
                step(side, k)

    take_near(main, 1)
    take_x(main, 0)

    @pl.when(cross)
    def _():
        to_far().wait_recv()
        for i in range(3):
            to_z(side, i).start()
        take_near(side, 0)

    take_x(main, 1)
    crossing((take_near, 1))
    take_near(main, 2)
    take_near(main, 3)
    crossing((take_x, 0))
    take_far(main, 0)
    crossing((take_x, 1), (take_near, 2), (take_near, 3))
    take_far(main, 1)
    take_x(main, 2)
    crossing((take_far, 0))
    take_x(main, 3)
    crossing((take_x, 2), (take_far, 1))
    take_far(main, 2)
    crossing((take_x, 3))
    z_group(0)
    z_group(1)
    take_far(main, 3)
    crossing((take_far, 2), (take_far, 3))
    z_group(2)
    z_group(3)

    load.wait()

    def to_ratio(z, blurred):
        ratio = obs[z] / blurred
        for b in range(4):
            rows = rat.at[b].reshape(3072, 128)
            rows[pl.ds(z + 16, 64, stride=48), :] = ratio[:, 128 * b : 128 * b + 128]

    def up_ratio(c):
        src, dst = (rat.at[:, :, pl.ds(o + 8 * c, 8), :] for o in (16, 0))
        return remote(src, dst, rup_send.at[c], rlo_recv.at[c], (v, s + 1))

    def dn_ratio(c):
        src, dst = (rat.at[:, :, pl.ds(o + 8 * c, 8), :] for o in (16, 32))
        return remote(src, dst, rdn_send.at[c], rhi_recv.at[c], (v, s - 1))

    def rows_of(off, c, first, count):
        return rat.at[:, pl.ds(first, count), pl.ds(pl.multiple_of(off + 8 * c, 8), 8), :]

    def far_ratio(c):
        src, dst = rows_of(16, c, 0, DIRECT), rows_of(far_off, c, 0, DIRECT)
        return remote(src, dst, far_send.at[1 + c], far_recv.at[1 + c], (v, far_slab))

    def to_relay(c, p):
        src = rows_of(16, c, DIRECT + PIECE * p, PIECE)
        return remote(src, relay.at[c, p], rel_send.at[c, p], rel_recv.at[c, p], (v, my_relay))

    def from_relay(c, p):
        dst = rows_of(jnp.where(bottom, 0, 32), c, DIRECT + PIECE * p, PIECE)
        return remote(relay.at[c, p], dst, fwd_send.at[c, p], fwd_recv.at[c, p], (v, relay_to))

    for c in range(2):
        x_stage(thi, tlo, cxf, exf, xo, c)
        y_stage(xo, wyf, to_ratio, c)

        @pl.when(cross)
        def _():
            to_relay(c, 0).start()
            to_relay(c, 1).start()
            far_ratio(c).start()

        @pl.when(near_hi)
        def _():
            up_ratio(c).start()

        @pl.when(near_lo)
        def _():
            dn_ratio(c).start()

    build_tables(pz, py, px, wzb, wyb, cxb, exb, True)

    for c in range(2):

        @pl.when(relays)
        def _():
            for p in range(2):
                to_relay(c, p).wait_recv()
                from_relay(c, p).start()

        @pl.when(near_lo)
        def _():
            up_ratio(c).wait_recv()

        @pl.when(near_hi)
        def _():
            dn_ratio(c).wait_recv()

        @pl.when(cross)
        def _():
            far_ratio(c).wait_recv()
            for p in range(2):
                from_relay(c, p).wait_recv()

    def ratio_rows(y):
        return jnp.concatenate([rat[b, y] for b in range(4)], axis=1)

    def z_back(n, _):
        z_rows(ratio_rows, wzb, thi, tlo, n * 16, 16)
        return 0

    lax.fori_loop(0, 64 // 16, z_back, 0)

    def to_log(z, back):
        logs[z] = jnp.log(back)

    def x_rows(j, c, first, count):
        start = pl.multiple_of(xs[j] * 16 + first, 8)
        return logs.at[pl.ds(4 * c, 4), pl.ds(start, count), :]

    def share_far(c, i):
        dst = pin.at[i, pl.ds(4 * c, 4)]
        return remote(x_rows(3, c, 8 - 8 * i, 8), dst, sp_send.at[c, i], sp_recv.at[c, i], (xpeer[i], s))

    def share_x(c, i):
        dst = xin.at[i, pl.ds(4 * c, 4)]
        return remote(x_rows(1 + i, c, 0, 16), dst, sx_send.at[c, i], sx_recv.at[c, i], (xpeer[i], s))

    def share_z(c, i):
        j = zs[i + 1]
        src = zout.at[j, pl.ds(16 * c, 16), :]
        return remote(src, zin.at[i, pl.ds(16 * c, 16), :], sz_send.at[c, i], sz_recv.at[c, i], (zpeer[i], s))

    def send_far(c):
        for i in range(2):
            share_far(c, i).start()

    def send_near(c):
        for i in range(2):
            share_far(c, i).wait_recv()
            j, first = 2 - i, 8 - 8 * i
            ref = x_rows(j, c, first, 8)
            ref[...] = ref[...] + pin[i, 4 * c : 4 * c + 4]
        for i in range(2):
            share_x(c, i).start()

    def reduce_x(c):
        for i in range(2):
            share_x(c, i).wait_recv()
        for q in range(4):
            z = 4 * c + q
            total = logs[z, pl.ds(pl.multiple_of(x * 16, 16), 16), :]
            for i in range(2):
                total = total + xin[i, z]
            for j in range(4):
                zout[j, 4 * z : 4 * z + 4, :] = total[4 * j : 4 * j + 4]
        for i in range(3):
            share_z(c, i).start()

    def final(c):
        for i in range(3):
            share_z(c, i).wait_recv()
        for q in range(4):
            z = 4 * c + q
            rows = pl.ds(4 * z, 4)
            total = zout[zl, rows, :]
            for i in range(3):
                total = total + zin[i, rows, :]
            out[z] = total

    x_stage(thi, tlo, cxb, exb, xo, 0)
    y_stage(xo, wyb, to_log, 0, 0, 4)
    send_far(0)
    y_stage(xo, wyb, to_log, 0, 4, 8)
    send_far(1)
    x_stage(thi, tlo, cxb, exb, xo, 1)
    send_near(0)
    y_stage(xo, wyb, to_log, 1, 0, 4)
    send_far(2)
    send_near(1)
    y_stage(xo, wyb, to_log, 1, 4, 8)
    send_far(3)
    send_near(2)
    reduce_x(0)
    send_near(3)
    for c in range(1, 4):
        reduce_x(c)
    for c in range(4):
        final(c)

    def drain(stream):
        for i in range(3):
            to_z(stream, i).wait_send()
        for i in range(2):
            for k in range(4):
                to_x(stream, i, k, v).wait_send()
                on_x(stream, i, k, v).wait_send()

    drain(main)
    for c in range(4):
        for i in range(2):
            share_far(c, i).wait_send()
            share_x(c, i).wait_send()
        for i in range(3):
            share_z(c, i).wait_send()

    @pl.when(cross)
    def _():
        drain(side)
        to_far().wait_send()
        for c in range(2):
            far_ratio(c).wait_send()
            to_relay(c, 0).wait_send()
            to_relay(c, 1).wait_send()

    @pl.when(relays)
    def _():
        for c in range(2):
            from_relay(c, 0).wait_send()
            from_relay(c, 1).wait_send()

    @pl.when(near_hi)
    def _():
        for k in range(16):
            to_up(v, k).wait_send()
        for c in range(2):
            up_ratio(c).wait_send()

    @pl.when(near_lo)
    def _():
        for k in range(16):
            to_dn(v, k).wait_send()
        for c in range(2):
            dn_ratio(c).wait_send()


TABLES = [
    pltpu.VMEM((96, 96), BF16),
    pltpu.VMEM((128, 384), BF16),
    pltpu.VMEM((3, 256, 256), BF16),
    pltpu.VMEM((3, 256, 256), BF16),
]
DMA = pltpu.SemaphoreType.DMA
SMEM = pl.BlockSpec(memory_space=pltpu.SMEM)
VM = pl.BlockSpec(memory_space=pltpu.VMEM)
ANY = pl.BlockSpec(memory_space=pl.ANY)


def local(estimate, observed, psf_z, psf_y, psf_x):
    taps = [jnp.swapaxes(p, 0, 1) for p in (psf_z, psf_y, psf_x)]
    share = pl.pallas_call(
        kernel,
        out_shape=jax.ShapeDtypeStruct(estimate.shape, F32),
        in_specs=[SMEM] * 3 + [VM, ANY],
        out_specs=VM,
        scratch_shapes=[
            pltpu.VMEM((64, 48, 512), F32),
            pltpu.VMEM((4, 64, 48, 128), F32),
            pltpu.VMEM((2, 2, 4, PIECE, 8, 128), F32),
            pltpu.VMEM((16, 64, 512), F32),
            pltpu.VMEM((2, 3, 512, 512), BF16),
            pltpu.VMEM((2, 3, 512, 512), BF16),
            pltpu.VMEM((2, 4, 1536, 128), F32),
            pltpu.VMEM((16, 64, 512), F32),
            pltpu.VMEM((2, 16, 8, 512), F32),
            pltpu.VMEM((2, 16, 16, 512), F32),
            pltpu.VMEM((4, 64, 512), F32),
            pltpu.VMEM((3, 64, 512), F32),
        ]
        + TABLES * 2
        + [DMA((1,))]
        + [DMA((16,))] * 4
        + [DMA((3,))] * 2
        + [DMA((3,)), DMA((3,)), DMA((2, 4)), DMA((2, 4)), DMA((2, 4)), DMA((2, 4))] * 2
        + [DMA((2,))] * 4
        + [DMA((2, 2))] * 4
        + [DMA((4, 2))] * 4
        + [DMA((4, 3))] * 2,
        compiler_params=pltpu.CompilerParams(
            collective_id=0, has_side_effects=True, vmem_limit_bytes=60 << 20
        ),
        name="deconvolve",
    )(*taps, estimate, observed[0])
    return estimate * jnp.exp(share)


def solution(mesh):
    placed = (
        P("slab", "view", None),
        P("view", "slab", None, None),
        P("view", None, None),
        P("view", None, None),
        P("view", None, None),
    )
    return jax.shard_map(
        local, mesh=mesh, in_specs=placed, out_specs=P("slab", "view", None), check_vma=False
    )
```

```python
import functools

import jax
import jax.numpy as jnp
from jax import lax
from jax.experimental import pallas as pl
from jax.experimental.pallas import tpu as pltpu
from jax.sharding import PartitionSpec as P

RANK = 3
TAPS = 31
HALF = 15
F32, BF16 = jnp.float32, jnp.bfloat16


def split(x):
    hi = x.astype(BF16)
    return hi, (x - hi.astype(F32)).astype(BF16)


def pick(code, count, tap):
    def one(k, acc):
        return jnp.where(code == k, tap(k), acc)

    return lax.fori_loop(0, count, one, jnp.zeros(code.shape, F32))


def iotas(shape):
    return [lax.broadcasted_iota(jnp.int32, shape, d) for d in range(2)]


def build_tables(pz, py, px, wz, wy, cx, ex, back):
    def tap_of(ref):
        return lambda k: ref[k // TAPS, 0, k % TAPS]

    row, col = iotas((48, 96))
    p = jnp.where(col < 48, col, col - 48)
    d = (row % 16) - p + 31 if back else p - (row % 16) - 1
    code = jnp.where((d >= 0) & (d < TAPS), (row // 16) * TAPS + d, -1)
    hi, lo = split(pick(code, RANK * TAPS, tap_of(pz)))
    wz[0:48, :] = hi
    wz[48:96, :] = jnp.where(col < 48, lo.astype(F32), 0.0).astype(BF16)

    row, col = iotas((64, 384))
    c = jnp.where(col < 192, col, col - 192)
    d = row - (c % 64) + HALF if back else (c % 64) - row + HALF
    code = jnp.where((d >= 0) & (d < TAPS), (c // 64) * TAPS + d, -1)
    hi, lo = split(pick(code, RANK * TAPS, tap_of(py)))
    wy[0:64, :] = hi
    wy[64:128, :] = jnp.where(col < 192, lo.astype(F32), 0.0).astype(BF16)

    row, col = iotas((128, 128))
    d = col - row + HALF if back else row - col + HALF
    ring = lax.rem(d + 128, 128)
    near = (d >= 0) & (d < TAPS)
    zero = jnp.zeros((128, 128), BF16)
    for r in range(RANK):
        full = pick(ring, TAPS, lambda k: px[r, 0, k])
        for ref, keep in ((cx, near), (ex, jnp.logical_not(near))):
            hi, lo = split(jnp.where(keep, full, 0.0))
            ref[r, 0:128, 0:128] = hi
            ref[r, 0:128, 128:256] = lo
            ref[r, 128:256, 0:128] = hi
            ref[r, 128:256, 128:256] = zero


def dot(a, b):
    return jnp.dot(a, b, preferred_element_type=F32)


def z_rows(load, wz, thi, tlo, start, count):
    for i in range(0, count, 2):
        pair = []
        for y in (start + i, start + i + 1):
            hi, lo = split(load(y))
            o = dot(wz[...], jnp.concatenate([hi, lo], axis=0))
            pair.append(o[:48] + o[48:])
        rows = pl.ds(pl.multiple_of((start + i) * 8, 16), 16)
        for h in range(2):
            for r in range(RANK):
                top = 16 * r + 8 * h
                hi, lo = split(jnp.concatenate([p[top : top + 8] for p in pair], axis=0))
                thi[h, r, rows, :] = hi
                tlo[h, r, rows, :] = lo


def x_stage(thi, tlo, cx, ex, xo, h, first=0, m=512):
    low = lax.broadcasted_iota(jnp.int32, (m, 128), 1) < 64

    for r in range(RANK):

        def one():
            rows = pl.ds(first, m)
            dest = pl.ds(r * 512 + first, m)

            def lanes(ref, b):
                return ref[h, r, rows, 128 * b : 128 * b + 128]

            before = jnp.zeros((m, 128), F32)
            for b in range(4):
                hi, lo = lanes(thi, b), lanes(tlo, b)
                o = dot(jnp.concatenate([hi, lo], axis=1), cx[r])
                after = jnp.zeros((m, 128), F32)
                if b < 3:
                    hi = jnp.where(low, lanes(thi, b + 1), hi)
                    lo = jnp.where(low, lanes(tlo, b + 1), lo)
                    e = dot(jnp.concatenate([hi, lo], axis=1), ex[r])
                    after = e[:, :128] + e[:, 128:]
                xo[h, b, dest, :] = o[:, :128] + o[:, 128:] + jnp.where(low, before, after)
                before = after

        one()


def y_stage(xo, wy, finish, h, lo=0, hi=8):
    def one(z, _):
        planes = []
        for r in range(RANK):
            parts = [xo[h, b, pl.ds(r * 512 + z, 64, stride=8), :] for b in range(4)]
            planes.append(jnp.concatenate(parts, axis=1))
        a, l = split(jnp.concatenate(planes, axis=0))
        o = dot(wy[...], jnp.concatenate([a, l], axis=0))
        finish(8 * h + z, o[:64] + o[64:])
        return 0

    lax.fori_loop(lo, hi, one, 0, unroll=4)


SLABS, GROUP = 16, 4
DIRECT, PIECE = 32, 16
CHUNKS, DEEP = 8, 2
PARTS = ((0, 0, 64), (1, 0, 32), (1, 32, 32))
MESH = pl.DeviceIdType.MESH


def remote(src, dst, send, recv, device):
    return pltpu.make_async_remote_copy(
        src_ref=src, dst_ref=dst, send_sem=send, recv_sem=recv, device_id=device, device_id_type=MESH
    )


def kernel(
    pz, py, px, est, obs_hbm, out,
    fld, rat, relay, obs, thi, tlo, xo, logs, pin, xin, zout, zin,
    wzf, wyf, cxf, exf, wzb, wyb, cxb, exb,
    obs_sem, lo_recv, hi_recv, upsend, dnsend, far_send, far_recv,
    mz_send, mz_recv, mx_send, mx_recv, mc_send, mc_recv,
    cz_send, cz_recv, cx_send, cx_recv, cc_send, cc_recv,
    rup_send, rdn_send, rlo_recv, rhi_recv,
    rel_send, rel_recv, fwd_send, fwd_recv,
    sp_send, sp_recv, sx_send, sx_recv, sz_send, sz_recv,
):
    v, s = lax.axis_index("view"), lax.axis_index("slab")
    x, zl = lax.div(v, GROUP), lax.rem(v, GROUP)
    zs = [zl, zl + 1 - 2 * lax.rem(zl, 2), lax.rem(zl + 2, GROUP), 3 - zl]
    xs = [x, x + 1 - 2 * lax.rem(x, 2), 3 - x, lax.rem(x + 2, GROUP)]
    zpeer = [x * GROUP + a for a in zs[1:]]
    xpeer = [a * GROUP + zl for a in xs[1:]]
    lower, upper = s > 0, s < SLABS - 1
    cross_lo, cross_hi = s == SLABS // 2, s == SLABS // 2 - 1
    cross = jnp.logical_or(cross_lo, cross_hi)
    near_lo = jnp.logical_and(lower, jnp.logical_not(cross_lo))
    near_hi = jnp.logical_and(upper, jnp.logical_not(cross_hi))
    my_off = pl.multiple_of(jnp.where(cross_lo, 0, 32), 16)
    far_off = pl.multiple_of(jnp.where(cross_lo, 32, 0), 16)
    far_slab = jnp.where(cross_lo, s - 1, s + 1)
    bottom, top = s == 0, s == SLABS - 1
    relays = jnp.logical_or(bottom, top)
    relay_to = jnp.where(bottom, SLABS // 2, SLABS // 2 - 1)
    my_relay = jnp.where(cross_lo, SLABS - 1, 0)

    def block(shard, off):
        return fld.at[pl.ds(shard * 4, 4), pl.ds(off, 16), :]

    for q in range(4):
        fld[v * 4 + q, 16:32, :] = est[:, q, :]

    barrier = pltpu.get_barrier_semaphore()
    for peer in zpeer + xpeer:
        pl.semaphore_signal(barrier, inc=1, device_id=(peer, s), device_id_type=MESH)

    @pl.when(lower)
    def _():
        pl.semaphore_signal(barrier, inc=1, device_id=(v, s - 1), device_id_type=MESH)

    @pl.when(upper)
    def _():
        pl.semaphore_signal(barrier, inc=1, device_id=(v, s + 1), device_id_type=MESH)

    @pl.when(relays)
    def _():
        for peer in (SLABS // 2 - 1, SLABS // 2):
            pl.semaphore_signal(barrier, inc=1, device_id=(v, peer), device_id_type=MESH)

    @pl.when(cross)
    def _():
        for peer in (0, SLABS - 1):
            pl.semaphore_signal(barrier, inc=1, device_id=(v, peer), device_id_type=MESH)

    extra = jnp.where(jnp.logical_or(relays, cross), 2, 0)
    pl.semaphore_wait(barrier, extra + 6 + jnp.where(lower, 1, 0) + jnp.where(upper, 1, 0))

    def shard(j, k):
        return xs[j] * GROUP + zs[k]

    def half(which, off, h):
        return fld.at[pl.ds(which * 4 + 2 * h, 2), pl.ds(off, 16), :]

    main = (16, mz_send, mz_recv, mx_send, mx_recv, mc_send, mc_recv)
    side = (my_off, cz_send, cz_recv, cx_send, cx_recv, cc_send, cc_recv)

    def to_z(stream, i):
        ref = block(v, stream[0])
        return remote(ref, ref, stream[1].at[i], stream[2].at[i], (zpeer[i], s))

    def to_x(stream, i, k, which):
        ref = block(which, stream[0])
        return remote(ref, ref, stream[3].at[i, k], stream[4].at[i, k], (xpeer[i], s))

    def on_x(stream, h, k, which):
        ref = half(which, stream[0], h)
        return remote(ref, ref, stream[5].at[h, k], stream[6].at[h, k], (xpeer[1 - h], s))

    def to_up(which, n):
        return remote(block(which, 16), block(which, 0), upsend.at[n], lo_recv.at[n], (v, s + 1))

    def to_dn(which, n):
        return remote(block(which, 16), block(which, 32), dnsend.at[n], hi_recv.at[n], (v, s - 1))

    def to_far():
        return remote(block(v, 16), block(v, far_off), far_send.at[0], far_recv.at[0], (v, far_slab))

    def halo(stream, j, k):
        if stream is main:

            @pl.when(near_hi)
            def _():
                to_up(shard(j, k), 4 * j + k).start()

            @pl.when(near_lo)
            def _():
                to_dn(shard(j, k), 4 * j + k).start()

    def take_near(stream, k):
        if k > 0:
            to_z(stream, k - 1).wait_recv()
        for i in range(2):
            to_x(stream, i, k, shard(0, k)).start()
        halo(stream, 0, k)

    def take_x(stream, k):
        for i in range(2):
            to_x(stream, i, k, shard(1 + i, k)).wait_recv()
            on_x(stream, i, k, shard(1 + i, k)).start()
            halo(stream, 1 + i, k)

    def take_far(stream, k):
        for h in range(2):
            on_x(stream, h, k, shard(3, k)).wait_recv()
        halo(stream, 3, k)

    @pl.when(cross)
    def _():
        to_far().start()

    for i in range(3):
        to_z(main, i).start()
    take_near(main, 0)
    load = pltpu.make_async_copy(obs_hbm, obs, obs_sem.at[0])
    load.start()

    @pl.when(s == 0)
    def _():
        fld[:, 0:16, :] = jnp.zeros((64, 16, 512), F32)
        rat[:, :, 0:16, :] = jnp.zeros((4, 64, 16, 128), F32)

    @pl.when(s == SLABS - 1)
    def _():
        fld[:, 32:48, :] = jnp.zeros((64, 16, 512), F32)
        rat[:, :, 32:48, :] = jnp.zeros((4, 64, 16, 128), F32)

    build_tables(pz, py, px, wzf, wyf, cxf, exf, False)

    def z_group(k):
        for j in range(4):

            @pl.when(near_lo)
            def _():
                to_up(v, 4 * j + k).wait_recv()

            @pl.when(near_hi)
            def _():
                to_dn(v, 4 * j + k).wait_recv()

        def one(j, _):
            first = lax.rem(xs[0] + j, GROUP) * GROUP + zs[k]
            z_rows(lambda y: fld[y], wzf, thi, tlo, first * 4, 4)
            return 0

        lax.fori_loop(0, GROUP, one, 0)

    def crossing(*steps):
        @pl.when(cross)
        def _():
            for step, k in steps:
                step(side, k)

    take_near(main, 1)
    take_x(main, 0)

    @pl.when(cross)
    def _():
        to_far().wait_recv()
        for i in range(3):
            to_z(side, i).start()
        take_near(side, 0)

    take_x(main, 1)
    crossing((take_near, 1))
    take_near(main, 2)
    take_near(main, 3)
    crossing((take_x, 0))
    take_far(main, 0)
    crossing((take_x, 1), (take_near, 2), (take_near, 3))
    take_far(main, 1)
    take_x(main, 2)
    crossing((take_far, 0))
    take_x(main, 3)
    crossing((take_x, 2), (take_far, 1))
    take_far(main, 2)
    crossing((take_x, 3))
    z_group(0)
    z_group(1)
    take_far(main, 3)
    crossing((take_far, 2), (take_far, 3))
    z_group(2)
    z_group(3)

    load.wait()

    def to_ratio(z, blurred):
        ratio = obs[z] / blurred
        for b in range(4):
            rows = rat.at[b].reshape(3072, 128)
            rows[pl.ds(z + 16, 64, stride=48), :] = ratio[:, 128 * b : 128 * b + 128]

    def slab_ratio(n, off, send, recv, slab):
        c, first, count = PARTS[n]
        src, dst = (rat.at[:, pl.ds(first, count), pl.ds(o + 8 * c, 8), :] for o in (16, off))
        return remote(src, dst, send.at[n], recv.at[n], (v, slab))

    def up_ratio(n):
        return slab_ratio(n, 0, rup_send, rlo_recv, s + 1)

    def dn_ratio(n):
        return slab_ratio(n, 32, rdn_send, rhi_recv, s - 1)

    def rows_of(off, c, first, count):
        return rat.at[:, pl.ds(first, count), pl.ds(pl.multiple_of(off + 8 * c, 8), 8), :]

    def far_ratio(c):
        src, dst = rows_of(16, c, 0, DIRECT), rows_of(far_off, c, 0, DIRECT)
        return remote(src, dst, far_send.at[1 + c], far_recv.at[1 + c], (v, far_slab))

    def to_relay(c, p):
        src = rows_of(16, c, DIRECT + PIECE * p, PIECE)
        return remote(src, relay.at[c, p], rel_send.at[c, p], rel_recv.at[c, p], (v, my_relay))

    def from_relay(c, p):
        dst = rows_of(jnp.where(bottom, 0, 32), c, DIRECT + PIECE * p, PIECE)
        return remote(relay.at[c, p], dst, fwd_send.at[c, p], fwd_recv.at[c, p], (v, relay_to))

    for c in range(2):
        x_stage(thi, tlo, cxf, exf, xo, c)
        y_stage(xo, wyf, to_ratio, c)

        @pl.when(cross)
        def _():
            to_relay(c, 0).start()
            to_relay(c, 1).start()
            far_ratio(c).start()

        @pl.when(near_hi)
        def _():
            for n in (0,) if c == 0 else (1, 2):
                up_ratio(n).start()

        @pl.when(near_lo)
        def _():
            for n in (0,) if c == 0 else (1, 2):
                dn_ratio(n).start()

    build_tables(pz, py, px, wzb, wyb, cxb, exb, True)

    @pl.when(relays)
    def _():
        for c in range(2):
            for p in range(2):
                to_relay(c, p).wait_recv()
                from_relay(c, p).start()

    def take_ratio(parts):
        @pl.when(near_lo)
        def _():
            for n in parts:
                up_ratio(n).wait_recv()

        @pl.when(near_hi)
        def _():
            for n in parts:
                dn_ratio(n).wait_recv()

    def ratio_rows(y):
        return jnp.concatenate([rat[b, y] for b in range(4)], axis=1)

    def z_back(n, _):
        z_rows(ratio_rows, wzb, thi, tlo, n * 16, 16)
        return 0

    take_ratio((0, 1))

    @pl.when(cross)
    def _():
        for c in range(2):
            far_ratio(c).wait_recv()
        for p in range(2):
            from_relay(0, p).wait_recv()

    lax.fori_loop(0, 2, z_back, 0)
    for h in range(2):
        x_stage(thi, tlo, cxb, exb, xo, h, 0, 256)
    take_ratio((2,))

    @pl.when(cross)
    def _():
        for p in range(2):
            from_relay(1, p).wait_recv()

    lax.fori_loop(2, 4, z_back, 0)

    def to_log(z, back):
        logs[z] = jnp.log(back)

    def x_rows(j, c, first, count):
        start = pl.multiple_of(xs[j] * 16 + first, 8)
        return logs.at[pl.ds(DEEP * c, DEEP), pl.ds(start, count), :]

    def share_far(c, i):
        dst = pin.at[i, pl.ds(DEEP * c, DEEP)]
        return remote(x_rows(3, c, 8 - 8 * i, 8), dst, sp_send.at[c, i], sp_recv.at[c, i], (xpeer[i], s))

    def share_x(c, i):
        dst = xin.at[i, pl.ds(DEEP * c, DEEP)]
        return remote(x_rows(1 + i, c, 0, 16), dst, sx_send.at[c, i], sx_recv.at[c, i], (xpeer[i], s))

    def share_z(c, i):
        j = zs[i + 1]
        src = zout.at[j, pl.ds(4 * DEEP * c, 4 * DEEP), :]
        return remote(src, zin.at[i, pl.ds(4 * DEEP * c, 4 * DEEP), :], sz_send.at[c, i], sz_recv.at[c, i], (zpeer[i], s))

    def send_far(c):
        for i in range(2):
            share_far(c, i).start()

    def send_near(c):
        for i in range(2):
            share_far(c, i).wait_recv()
            j, first = 2 - i, 8 - 8 * i
            ref = x_rows(j, c, first, 8)
            ref[...] = ref[...] + pin[i, DEEP * c : DEEP * c + DEEP]
        for i in range(2):
            share_x(c, i).start()

    def reduce_x(c):
        for i in range(2):
            share_x(c, i).wait_recv()
        for q in range(DEEP):
            z = DEEP * c + q
            total = logs[z, pl.ds(pl.multiple_of(x * 16, 16), 16), :]
            for i in range(2):
                total = total + xin[i, z]
            for j in range(4):
                zout[j, 4 * z : 4 * z + 4, :] = total[4 * j : 4 * j + 4]
        for i in range(3):
            share_z(c, i).start()

    def final(c):
        for i in range(3):
            share_z(c, i).wait_recv()
        for q in range(DEEP):
            z = DEEP * c + q
            rows = pl.ds(4 * z, 4)
            total = zout[zl, rows, :]
            for i in range(3):
                total = total + zin[i, rows, :]
            out[z] = total

    x_stage(thi, tlo, cxb, exb, xo, 0, 256, 256)
    y_stage(xo, wyb, to_log, 0, 0, 4)
    send_far(0)
    send_far(1)
    y_stage(xo, wyb, to_log, 0, 4, 8)
    send_far(2)
    send_far(3)
    x_stage(thi, tlo, cxb, exb, xo, 1, 256, 256)
    send_near(0)
    send_near(1)
    y_stage(xo, wyb, to_log, 1, 0, 4)
    send_far(4)
    send_far(5)
    send_near(2)
    send_near(3)
    y_stage(xo, wyb, to_log, 1, 4, 8)
    send_far(6)
    send_far(7)
    for c in range(4, CHUNKS):
        send_near(c)
        reduce_x(c - 4)
    for c in range(4, CHUNKS):
        reduce_x(c)
    for c in range(CHUNKS):
        final(c)

    def drain(stream):
        for i in range(3):
            to_z(stream, i).wait_send()
        for i in range(2):
            for k in range(4):
                to_x(stream, i, k, v).wait_send()
                on_x(stream, i, k, v).wait_send()

    drain(main)
    for c in range(CHUNKS):
        for i in range(2):
            share_far(c, i).wait_send()
            share_x(c, i).wait_send()
        for i in range(3):
            share_z(c, i).wait_send()

    @pl.when(cross)
    def _():
        drain(side)
        to_far().wait_send()
        for c in range(2):
            far_ratio(c).wait_send()
            to_relay(c, 0).wait_send()
            to_relay(c, 1).wait_send()

    @pl.when(relays)
    def _():
        for c in range(2):
            from_relay(c, 0).wait_send()
            from_relay(c, 1).wait_send()

    @pl.when(near_hi)
    def _():
        for k in range(16):
            to_up(v, k).wait_send()
        for n in range(3):
            up_ratio(n).wait_send()

    @pl.when(near_lo)
    def _():
        for k in range(16):
            to_dn(v, k).wait_send()
        for n in range(3):
            dn_ratio(n).wait_send()


TABLES = [
    pltpu.VMEM((96, 96), BF16),
    pltpu.VMEM((128, 384), BF16),
    pltpu.VMEM((3, 256, 256), BF16),
    pltpu.VMEM((3, 256, 256), BF16),
]
DMA = pltpu.SemaphoreType.DMA
SMEM = pl.BlockSpec(memory_space=pltpu.SMEM)
VM = pl.BlockSpec(memory_space=pltpu.VMEM)
ANY = pl.BlockSpec(memory_space=pl.ANY)


def local(estimate, observed, psf_z, psf_y, psf_x):
    taps = [jnp.swapaxes(p, 0, 1) for p in (psf_z, psf_y, psf_x)]
    share = pl.pallas_call(
        kernel,
        out_shape=jax.ShapeDtypeStruct(estimate.shape, F32),
        in_specs=[SMEM] * 3 + [VM, ANY],
        out_specs=VM,
        scratch_shapes=[
            pltpu.VMEM((64, 48, 512), F32),
            pltpu.VMEM((4, 64, 48, 128), F32),
            pltpu.VMEM((2, 2, 4, PIECE, 8, 128), F32),
            pltpu.VMEM((16, 64, 512), F32),
            pltpu.VMEM((2, 3, 512, 512), BF16),
            pltpu.VMEM((2, 3, 512, 512), BF16),
            pltpu.VMEM((2, 4, 1536, 128), F32),
            pltpu.VMEM((16, 64, 512), F32),
            pltpu.VMEM((2, 16, 8, 512), F32),
            pltpu.VMEM((2, 16, 16, 512), F32),
            pltpu.VMEM((4, 64, 512), F32),
            pltpu.VMEM((3, 64, 512), F32),
        ]
        + TABLES * 2
        + [DMA((1,))]
        + [DMA((16,))] * 4
        + [DMA((3,))] * 2
        + [DMA((3,)), DMA((3,)), DMA((2, 4)), DMA((2, 4)), DMA((2, 4)), DMA((2, 4))] * 2
        + [DMA((3,))] * 4
        + [DMA((2, 2))] * 4
        + [DMA((CHUNKS, 2))] * 4
        + [DMA((CHUNKS, 3))] * 2,
        compiler_params=pltpu.CompilerParams(
            collective_id=0, has_side_effects=True, vmem_limit_bytes=60 << 20
        ),
        name="deconvolve",
    )(*taps, estimate, observed[0])
    return estimate * jnp.exp(share)


def solution(mesh):
    placed = (
        P("slab", "view", None),
        P("view", "slab", None, None),
        P("view", None, None),
        P("view", None, None),
        P("view", None, None),
    )
    return jax.shard_map(
        local, mesh=mesh, in_specs=placed, out_specs=P("slab", "view", None), check_vma=False
    )
```

```python
import functools

import jax
import jax.numpy as jnp
from jax import lax
from jax.experimental import pallas as pl
from jax.experimental.pallas import tpu as pltpu
from jax.sharding import PartitionSpec as P

RANK = 3
TAPS = 31
HALF = 15
F32, BF16 = jnp.float32, jnp.bfloat16


def split(x):
    hi = x.astype(BF16)
    return hi, (x - hi.astype(F32)).astype(BF16)


def pick(code, count, tap):
    def one(k, acc):
        return jnp.where(code == k, tap(k), acc)

    return lax.fori_loop(0, count, one, jnp.zeros(code.shape, F32))


def iotas(shape):
    return [lax.broadcasted_iota(jnp.int32, shape, d) for d in range(2)]


def build_tables(pz, py, px, wz, wy, cx, ex, back):
    def tap_of(ref):
        return lambda k: ref[k // TAPS, 0, k % TAPS]

    row, col = iotas((48, 96))
    p = jnp.where(col < 48, col, col - 48)
    d = (row % 16) - p + 31 if back else p - (row % 16) - 1
    code = jnp.where((d >= 0) & (d < TAPS), (row // 16) * TAPS + d, -1)
    hi, lo = split(pick(code, RANK * TAPS, tap_of(pz)))
    wz[0:48, :] = hi
    wz[48:96, :] = jnp.where(col < 48, lo.astype(F32), 0.0).astype(BF16)

    row, col = iotas((64, 384))
    c = jnp.where(col < 192, col, col - 192)
    d = row - (c % 64) + HALF if back else (c % 64) - row + HALF
    code = jnp.where((d >= 0) & (d < TAPS), (c // 64) * TAPS + d, -1)
    hi, lo = split(pick(code, RANK * TAPS, tap_of(py)))
    wy[0:64, :] = hi
    wy[64:128, :] = jnp.where(col < 192, lo.astype(F32), 0.0).astype(BF16)

    row, col = iotas((128, 128))
    d = col - row + HALF if back else row - col + HALF
    ring = lax.rem(d + 128, 128)
    near = (d >= 0) & (d < TAPS)
    zero = jnp.zeros((128, 128), BF16)
    for r in range(RANK):
        full = pick(ring, TAPS, lambda k: px[r, 0, k])
        for ref, keep in ((cx, near), (ex, jnp.logical_not(near))):
            hi, lo = split(jnp.where(keep, full, 0.0))
            ref[r, 0:128, 0:128] = hi
            ref[r, 0:128, 128:256] = lo
            ref[r, 128:256, 0:128] = hi
            ref[r, 128:256, 128:256] = zero


def dot(a, b):
    return jnp.dot(a, b, preferred_element_type=F32)


def z_rows(load, wz, thi, tlo, start, count):
    for i in range(0, count, 2):
        pair = []
        for y in (start + i, start + i + 1):
            hi, lo = split(load(y))
            o = dot(wz[...], jnp.concatenate([hi, lo], axis=0))
            pair.append(o[:48] + o[48:])
        rows = pl.ds(pl.multiple_of((start + i) * 8, 16), 16)
        for h in range(2):
            for r in range(RANK):
                top = 16 * r + 8 * h
                hi, lo = split(jnp.concatenate([p[top : top + 8] for p in pair], axis=0))
                thi[h, r, rows, :] = hi
                tlo[h, r, rows, :] = lo


def x_stage(thi, tlo, cx, ex, xo, h, first=0, m=512):
    low = lax.broadcasted_iota(jnp.int32, (m, 128), 1) < 64

    for r in range(RANK):

        def one():
            rows = pl.ds(first, m)
            dest = pl.ds(r * 512 + first, m)

            def lanes(ref, b):
                return ref[h, r, rows, 128 * b : 128 * b + 128]

            before = jnp.zeros((m, 128), F32)
            for b in range(4):
                hi, lo = lanes(thi, b), lanes(tlo, b)
                o = dot(jnp.concatenate([hi, lo], axis=1), cx[r])
                after = jnp.zeros((m, 128), F32)
                if b < 3:
                    hi = jnp.where(low, lanes(thi, b + 1), hi)
                    lo = jnp.where(low, lanes(tlo, b + 1), lo)
                    e = dot(jnp.concatenate([hi, lo], axis=1), ex[r])
                    after = e[:, :128] + e[:, 128:]
                xo[h, b, dest, :] = o[:, :128] + o[:, 128:] + jnp.where(low, before, after)
                before = after

        one()


def y_stage(xo, wy, finish, h, lo=0, hi=8):
    def one(z, _):
        planes = []
        for r in range(RANK):
            parts = [xo[h, b, pl.ds(r * 512 + z, 64, stride=8), :] for b in range(4)]
            planes.append(jnp.concatenate(parts, axis=1))
        a, l = split(jnp.concatenate(planes, axis=0))
        o = dot(wy[...], jnp.concatenate([a, l], axis=0))
        finish(8 * h + z, o[:64] + o[64:])
        return 0

    lax.fori_loop(lo, hi, one, 0, unroll=4)


SLABS, GROUP = 16, 4
DIRECT, PIECE, PIECES = 32, 8, 4
CHUNKS, DEEP = 8, 2
PARTS = ((0, 0, 64), (1, 0, 32), (1, 32, 32))
MESH = pl.DeviceIdType.MESH


def remote(src, dst, send, recv, device):
    return pltpu.make_async_remote_copy(
        src_ref=src, dst_ref=dst, send_sem=send, recv_sem=recv, device_id=device, device_id_type=MESH
    )


def kernel(
    pz, py, px, est, obs_hbm, out,
    fld, rat, relay, obs, thi, tlo, xo, logs, pin, xin, zout, zin,
    wzf, wyf, cxf, exf, wzb, wyb, cxb, exb,
    obs_sem, lo_recv, hi_recv, upsend, dnsend, far_send, far_recv,
    mz_send, mz_recv, mx_send, mx_recv, mc_send, mc_recv,
    cz_send, cz_recv, cx_send, cx_recv, cc_send, cc_recv,
    rup_send, rdn_send, rlo_recv, rhi_recv,
    rel_send, rel_recv, fwd_send, fwd_recv,
    sp_send, sp_recv, sx_send, sx_recv, sz_send, sz_recv,
):
    v, s = lax.axis_index("view"), lax.axis_index("slab")
    x, zl = lax.div(v, GROUP), lax.rem(v, GROUP)
    zs = [zl, zl + 1 - 2 * lax.rem(zl, 2), lax.rem(zl + 2, GROUP), 3 - zl]
    xs = [x, x + 1 - 2 * lax.rem(x, 2), 3 - x, lax.rem(x + 2, GROUP)]
    zpeer = [x * GROUP + a for a in zs[1:]]
    xpeer = [a * GROUP + zl for a in xs[1:]]
    lower, upper = s > 0, s < SLABS - 1
    cross_lo, cross_hi = s == SLABS // 2, s == SLABS // 2 - 1
    cross = jnp.logical_or(cross_lo, cross_hi)
    near_lo = jnp.logical_and(lower, jnp.logical_not(cross_lo))
    near_hi = jnp.logical_and(upper, jnp.logical_not(cross_hi))
    my_off = pl.multiple_of(jnp.where(cross_lo, 0, 32), 16)
    far_off = pl.multiple_of(jnp.where(cross_lo, 32, 0), 16)
    far_slab = jnp.where(cross_lo, s - 1, s + 1)
    bottom, top = s == 0, s == SLABS - 1
    relays = jnp.logical_or(bottom, top)
    relay_to = jnp.where(bottom, SLABS // 2, SLABS // 2 - 1)
    my_relay = jnp.where(cross_lo, SLABS - 1, 0)

    def block(shard, off):
        return fld.at[pl.ds(shard * 4, 4), pl.ds(off, 16), :]

    for q in range(4):
        fld[v * 4 + q, 16:32, :] = est[:, q, :]

    barrier = pltpu.get_barrier_semaphore()
    for peer in zpeer + xpeer:
        pl.semaphore_signal(barrier, inc=1, device_id=(peer, s), device_id_type=MESH)

    @pl.when(lower)
    def _():
        pl.semaphore_signal(barrier, inc=1, device_id=(v, s - 1), device_id_type=MESH)

    @pl.when(upper)
    def _():
        pl.semaphore_signal(barrier, inc=1, device_id=(v, s + 1), device_id_type=MESH)

    @pl.when(relays)
    def _():
        for peer in (SLABS // 2 - 1, SLABS // 2):
            pl.semaphore_signal(barrier, inc=1, device_id=(v, peer), device_id_type=MESH)

    @pl.when(cross)
    def _():
        for peer in (0, SLABS - 1):
            pl.semaphore_signal(barrier, inc=1, device_id=(v, peer), device_id_type=MESH)

    extra = jnp.where(jnp.logical_or(relays, cross), 2, 0)
    pl.semaphore_wait(barrier, extra + 6 + jnp.where(lower, 1, 0) + jnp.where(upper, 1, 0))

    def shard(j, k):
        return xs[j] * GROUP + zs[k]

    def half(which, off, h):
        return fld.at[pl.ds(which * 4 + 2 * h, 2), pl.ds(off, 16), :]

    main = (16, mz_send, mz_recv, mx_send, mx_recv, mc_send, mc_recv)
    side = (my_off, cz_send, cz_recv, cx_send, cx_recv, cc_send, cc_recv)

    def to_z(stream, i):
        ref = block(v, stream[0])
        return remote(ref, ref, stream[1].at[i], stream[2].at[i], (zpeer[i], s))

    def to_x(stream, i, k, which):
        ref = block(which, stream[0])
        return remote(ref, ref, stream[3].at[i, k], stream[4].at[i, k], (xpeer[i], s))

    def on_x(stream, h, k, which):
        ref = half(which, stream[0], h)
        return remote(ref, ref, stream[5].at[h, k], stream[6].at[h, k], (xpeer[1 - h], s))

    def to_up(which, n):
        return remote(block(which, 16), block(which, 0), upsend.at[n], lo_recv.at[n], (v, s + 1))

    def to_dn(which, n):
        return remote(block(which, 16), block(which, 32), dnsend.at[n], hi_recv.at[n], (v, s - 1))

    def to_far():
        return remote(block(v, 16), block(v, far_off), far_send.at[0], far_recv.at[0], (v, far_slab))

    def halo(stream, j, k):
        if stream is main:

            @pl.when(near_hi)
            def _():
                to_up(shard(j, k), 4 * j + k).start()

            @pl.when(near_lo)
            def _():
                to_dn(shard(j, k), 4 * j + k).start()

    def take_near(stream, k):
        if k > 0:
            to_z(stream, k - 1).wait_recv()
        for i in range(2):
            to_x(stream, i, k, shard(0, k)).start()
        halo(stream, 0, k)

    def take_x(stream, k):
        for i in range(2):
            to_x(stream, i, k, shard(1 + i, k)).wait_recv()
            on_x(stream, i, k, shard(1 + i, k)).start()
            halo(stream, 1 + i, k)

    def take_far(stream, k):
        for h in range(2):
            on_x(stream, h, k, shard(3, k)).wait_recv()
        halo(stream, 3, k)

    @pl.when(cross)
    def _():
        to_far().start()

    for i in range(3):
        to_z(main, i).start()
    take_near(main, 0)
    load = pltpu.make_async_copy(obs_hbm, obs, obs_sem.at[0])
    load.start()

    @pl.when(s == 0)
    def _():
        fld[:, 0:16, :] = jnp.zeros((64, 16, 512), F32)
        rat[:, :, 0:16, :] = jnp.zeros((4, 64, 16, 128), F32)

    @pl.when(s == SLABS - 1)
    def _():
        fld[:, 32:48, :] = jnp.zeros((64, 16, 512), F32)
        rat[:, :, 32:48, :] = jnp.zeros((4, 64, 16, 128), F32)

    build_tables(pz, py, px, wzf, wyf, cxf, exf, False)

    def z_group(k):
        for j in range(4):

            @pl.when(near_lo)
            def _():
                to_up(v, 4 * j + k).wait_recv()

            @pl.when(near_hi)
            def _():
                to_dn(v, 4 * j + k).wait_recv()

        def one(j, _):
            first = lax.rem(xs[0] + j, GROUP) * GROUP + zs[k]
            z_rows(lambda y: fld[y], wzf, thi, tlo, first * 4, 4)
            return 0

        lax.fori_loop(0, GROUP, one, 0)

    def crossing(*steps):
        @pl.when(cross)
        def _():
            for step, k in steps:
                step(side, k)

    take_near(main, 1)
    take_x(main, 0)

    @pl.when(cross)
    def _():
        to_far().wait_recv()
        for i in range(3):
            to_z(side, i).start()
        take_near(side, 0)

    take_x(main, 1)
    crossing((take_near, 1))
    take_near(main, 2)
    take_near(main, 3)
    crossing((take_x, 0))
    take_far(main, 0)
    crossing((take_x, 1), (take_near, 2), (take_near, 3))
    take_far(main, 1)
    take_x(main, 2)
    crossing((take_far, 0))
    take_x(main, 3)
    crossing((take_x, 2), (take_far, 1))
    take_far(main, 2)
    crossing((take_x, 3))
    z_group(0)
    take_far(main, 3)
    z_group(1)
    crossing((take_far, 2))
    z_group(2)
    crossing((take_far, 3))
    z_group(3)

    load.wait()

    def to_ratio(z, blurred):
        ratio = obs[z] / blurred
        for b in range(4):
            rows = rat.at[b].reshape(3072, 128)
            rows[pl.ds(z + 16, 64, stride=48), :] = ratio[:, 128 * b : 128 * b + 128]

    def slab_ratio(n, off, send, recv, slab):
        c, first, count = PARTS[n]
        src, dst = (rat.at[:, pl.ds(first, count), pl.ds(o + 8 * c, 8), :] for o in (16, off))
        return remote(src, dst, send.at[n], recv.at[n], (v, slab))

    def up_ratio(n):
        return slab_ratio(n, 0, rup_send, rlo_recv, s + 1)

    def dn_ratio(n):
        return slab_ratio(n, 32, rdn_send, rhi_recv, s - 1)

    def rows_of(off, c, first, count):
        return rat.at[:, pl.ds(first, count), pl.ds(pl.multiple_of(off + 8 * c, 8), 8), :]

    def far_ratio(c):
        src, dst = rows_of(16, c, 0, DIRECT), rows_of(far_off, c, 0, DIRECT)
        return remote(src, dst, far_send.at[1 + c], far_recv.at[1 + c], (v, far_slab))

    def to_relay(c, p):
        src = rows_of(16, c, DIRECT + PIECE * p, PIECE)
        return remote(src, relay.at[c, p], rel_send.at[c, p], rel_recv.at[c, p], (v, my_relay))

    def from_relay(c, p):
        dst = rows_of(jnp.where(bottom, 0, 32), c, DIRECT + PIECE * p, PIECE)
        return remote(relay.at[c, p], dst, fwd_send.at[c, p], fwd_recv.at[c, p], (v, relay_to))

    for c in range(2):
        x_stage(thi, tlo, cxf, exf, xo, c)
        y_stage(xo, wyf, to_ratio, c)

        @pl.when(cross)
        def _():
            for p in range(PIECES):
                to_relay(c, p).start()
            far_ratio(c).start()

        @pl.when(near_hi)
        def _():
            for n in (0,) if c == 0 else (1, 2):
                up_ratio(n).start()

        @pl.when(near_lo)
        def _():
            for n in (0,) if c == 0 else (1, 2):
                dn_ratio(n).start()

    build_tables(pz, py, px, wzb, wyb, cxb, exb, True)

    @pl.when(relays)
    def _():
        for c in range(2):
            for p in range(PIECES):
                to_relay(c, p).wait_recv()
                from_relay(c, p).start()

    def take_ratio(parts):
        @pl.when(near_lo)
        def _():
            for n in parts:
                up_ratio(n).wait_recv()

        @pl.when(near_hi)
        def _():
            for n in parts:
                dn_ratio(n).wait_recv()

    def ratio_rows(y):
        return jnp.concatenate([rat[b, y] for b in range(4)], axis=1)

    def z_back(n, _):
        z_rows(ratio_rows, wzb, thi, tlo, n * 16, 16)
        return 0

    take_ratio((0, 1))

    @pl.when(cross)
    def _():
        for c in range(2):
            far_ratio(c).wait_recv()
        for p in range(PIECES):
            from_relay(0, p).wait_recv()

    lax.fori_loop(0, 2, z_back, 0)
    for h in range(2):
        x_stage(thi, tlo, cxb, exb, xo, h, 0, 256)
    take_ratio((2,))

    @pl.when(cross)
    def _():
        for p in range(PIECES):
            from_relay(1, p).wait_recv()

    lax.fori_loop(2, 4, z_back, 0)

    def to_log(z, back):
        logs[z] = jnp.log(back)

    def x_rows(j, c, first, count):
        start = pl.multiple_of(xs[j] * 16 + first, 8)
        return logs.at[pl.ds(DEEP * c, DEEP), pl.ds(start, count), :]

    def share_far(c, i):
        dst = pin.at[i, pl.ds(DEEP * c, DEEP)]
        return remote(x_rows(3, c, 8 - 8 * i, 8), dst, sp_send.at[c, i], sp_recv.at[c, i], (xpeer[i], s))

    def share_x(c, i):
        dst = xin.at[i, pl.ds(DEEP * c, DEEP)]
        return remote(x_rows(1 + i, c, 0, 16), dst, sx_send.at[c, i], sx_recv.at[c, i], (xpeer[i], s))

    def share_z(c, i):
        j = zs[i + 1]
        src = zout.at[j, pl.ds(4 * DEEP * c, 4 * DEEP), :]
        return remote(src, zin.at[i, pl.ds(4 * DEEP * c, 4 * DEEP), :], sz_send.at[c, i], sz_recv.at[c, i], (zpeer[i], s))

    def send_far(c):
        for i in range(2):
            share_far(c, i).start()

    def send_near(c):
        for i in range(2):
            share_far(c, i).wait_recv()
            j, first = 2 - i, 8 - 8 * i
            ref = x_rows(j, c, first, 8)
            ref[...] = ref[...] + pin[i, DEEP * c : DEEP * c + DEEP]
        for i in range(2):
            share_x(c, i).start()

    def reduce_x(c):
        for i in range(2):
            share_x(c, i).wait_recv()
        for q in range(DEEP):
            z = DEEP * c + q
            total = logs[z, pl.ds(pl.multiple_of(x * 16, 16), 16), :]
            for i in range(2):
                total = total + xin[i, z]
            for j in range(4):
                zout[j, 4 * z : 4 * z + 4, :] = total[4 * j : 4 * j + 4]
        for i in range(3):
            share_z(c, i).start()

    def final(c):
        for i in range(3):
            share_z(c, i).wait_recv()
        for q in range(DEEP):
            z = DEEP * c + q
            rows = pl.ds(4 * z, 4)
            total = zout[zl, rows, :]
            for i in range(3):
                total = total + zin[i, rows, :]
            out[z] = total

    x_stage(thi, tlo, cxb, exb, xo, 0, 256, 256)
    y_stage(xo, wyb, to_log, 0, 0, 4)
    send_far(0)
    send_far(1)
    y_stage(xo, wyb, to_log, 0, 4, 8)
    send_far(2)
    send_far(3)
    x_stage(thi, tlo, cxb, exb, xo, 1, 256, 256)
    send_near(0)
    send_near(1)
    y_stage(xo, wyb, to_log, 1, 0, 4)
    send_far(4)
    send_far(5)
    send_near(2)
    send_near(3)
    y_stage(xo, wyb, to_log, 1, 4, 8)
    send_far(6)
    send_far(7)
    for c in range(4, CHUNKS):
        send_near(c)
        reduce_x(c - 4)
    for c in range(4, CHUNKS):
        reduce_x(c)
    for c in range(CHUNKS):
        final(c)

    def drain(stream):
        for i in range(3):
            to_z(stream, i).wait_send()
        for i in range(2):
            for k in range(4):
                to_x(stream, i, k, v).wait_send()
                on_x(stream, i, k, v).wait_send()

    drain(main)
    for c in range(CHUNKS):
        for i in range(2):
            share_far(c, i).wait_send()
            share_x(c, i).wait_send()
        for i in range(3):
            share_z(c, i).wait_send()

    @pl.when(cross)
    def _():
        drain(side)
        to_far().wait_send()
        for c in range(2):
            far_ratio(c).wait_send()
            for p in range(PIECES):
                to_relay(c, p).wait_send()

    @pl.when(relays)
    def _():
        for c in range(2):
            for p in range(PIECES):
                from_relay(c, p).wait_send()

    @pl.when(near_hi)
    def _():
        for k in range(16):
            to_up(v, k).wait_send()
        for n in range(3):
            up_ratio(n).wait_send()

    @pl.when(near_lo)
    def _():
        for k in range(16):
            to_dn(v, k).wait_send()
        for n in range(3):
            dn_ratio(n).wait_send()


TABLES = [
    pltpu.VMEM((96, 96), BF16),
    pltpu.VMEM((128, 384), BF16),
    pltpu.VMEM((3, 256, 256), BF16),
    pltpu.VMEM((3, 256, 256), BF16),
]
DMA = pltpu.SemaphoreType.DMA
SMEM = pl.BlockSpec(memory_space=pltpu.SMEM)
VM = pl.BlockSpec(memory_space=pltpu.VMEM)
ANY = pl.BlockSpec(memory_space=pl.ANY)


def local(estimate, observed, psf_z, psf_y, psf_x):
    taps = [jnp.swapaxes(p, 0, 1) for p in (psf_z, psf_y, psf_x)]
    share = pl.pallas_call(
        kernel,
        out_shape=jax.ShapeDtypeStruct(estimate.shape, F32),
        in_specs=[SMEM] * 3 + [VM, ANY],
        out_specs=VM,
        scratch_shapes=[
            pltpu.VMEM((64, 48, 512), F32),
            pltpu.VMEM((4, 64, 48, 128), F32),
            pltpu.VMEM((2, PIECES, 4, PIECE, 8, 128), F32),
            pltpu.VMEM((16, 64, 512), F32),
            pltpu.VMEM((2, 3, 512, 512), BF16),
            pltpu.VMEM((2, 3, 512, 512), BF16),
            pltpu.VMEM((2, 4, 1536, 128), F32),
            pltpu.VMEM((16, 64, 512), F32),
            pltpu.VMEM((2, 16, 8, 512), F32),
            pltpu.VMEM((2, 16, 16, 512), F32),
            pltpu.VMEM((4, 64, 512), F32),
            pltpu.VMEM((3, 64, 512), F32),
        ]
        + TABLES * 2
        + [DMA((1,))]
        + [DMA((16,))] * 4
        + [DMA((3,))] * 2
        + [DMA((3,)), DMA((3,)), DMA((2, 4)), DMA((2, 4)), DMA((2, 4)), DMA((2, 4))] * 2
        + [DMA((3,))] * 4
        + [DMA((2, PIECES))] * 4
        + [DMA((CHUNKS, 2))] * 4
        + [DMA((CHUNKS, 3))] * 2,
        compiler_params=pltpu.CompilerParams(
            collective_id=0, has_side_effects=True, vmem_limit_bytes=60 << 20
        ),
        name="deconvolve",
    )(*taps, estimate, observed[0])
    return estimate * jnp.exp(share)


def solution(mesh):
    placed = (
        P("slab", "view", None),
        P("view", "slab", None, None),
        P("view", None, None),
        P("view", None, None),
        P("view", None, None),
    )
    return jax.shard_map(
        local, mesh=mesh, in_specs=placed, out_specs=P("slab", "view", None), check_vma=False
    )
```
